256 devices in a mesh: gx: 8 (over x, core), gy: 8 (over z), body: 4 (over y).
Axes of the slice: x: 4, y: 4, z: 8, core: 2. Of those that a mesh axis runs over, the one named last changes fastest.
Arguments:
- fluid_position: float32 [32, 2, 256, 128], P('gx', None, ('gy', 'body')), may hold values from 0 to 1
- fluid_velocity: float32 [32, 2, 256, 128], P('gx', None, ('gy', 'body')), may hold values from -3 to 3
- fluid_volume: float32 [32, 256, 128], P('gx', ('gy', 'body')), may hold values from 0.5 to 2
- bound_offset: float32 [2, 262144], P(None, ('gx', 'gy', 'body')), may hold values from 0 to 1
- bound_cell: int32 [2, 262144], P(None, ('gx', 'gy', 'body')), may hold values from 0 to 255, as said below
- bound_body: int32 [262144], P(('gx', 'gy', 'body')), may hold values from 0 to 1023, as said below
- body_state: float32 [5, 1024], P(None, 'body')
- mass_inverse: float32 [1024], P('body'), may hold values from 0.02 to 0.2
- inertia_inverse: float32 [1024], P('body'), may hold values from 0.002 to 0.02
Outputs:
- new_position: float32 [32, 2, 256, 128], P('gx', None, ('gy', 'body'))
- new_velocity: float32 [32, 2, 256, 128], P('gx', None, ('gy', 'body'))
- fluid_depth: float32 [32, 256, 128], P('gx', ('gy', 'body'))
- body_motion: float32 [3, 1024], P(None, 'body')
- bound_velocity: float32 [2, 262144], P(None, ('gx', 'gy', 'body'))
The draws below stay inside these ranges and needn't reach their ends.
Inputs may be any that keep to these rules, and one draw needn't show every extreme that they name: `bound_cell`: device f in the order gx, gy, body holds boundary particles f * 1024 to (f + 1) * 1024 - 1, which lie in its own tile: blocks 4 (f // 32) to that + 3 along x and 8 (f % 32) to that + 7 along y. `bound_body`: every body has boundary particles; each boundary particle of device f belongs to a body of device f or of its neighbour along y (f + 1, or f - 1 for the last tile along y).
All inputs are finite; a program needn't handle non-finite values.
Results may differ from the reference program's by a relative error of at most 0.0003.
Values sent between devices are 32-bit elements; how exact they have to be, the bound alone decides.
No kernel may reach another device: no remote copies, remote signals or barrier semaphores. Data moves between devices by JAX's collectives and lax.ppermute only.
A program may use at most 128 MiB of HBM per device.

```python
import math
import jax
import jax.numpy as jnp
import numpy as np
from jax import lax

P_SIZE = 128
CBX = 4
CBY = 8
SUBSTEPS = 3
BODY_DEV = 4
NBX = 32
NBY = 256
NBODY = 1024
BPD = 1024
BTOT = 262144
N_GY = 8
N_BODY = 4


def draw_bound_cell(key, part):
    index_all = jnp.arange(BTOT, dtype=jnp.int32)
    device_of = index_all // BPD
    slot_of = index_all % BPD
    tiles_north = N_GY * N_BODY
    tile_east = device_of // tiles_north
    tile_north = device_of % tiles_north
    key_east, key_north = jax.random.split(key)
    step_east = jax.random.randint(key_east, (BTOT,), 0, CBX)
    step_north = jax.random.randint(key_north, (BTOT,), 0, CBY)
    step_east = jnp.where(slot_of == 0, 0, jnp.where(slot_of == BPD - 1, CBX - 1, step_east))
    step_north = jnp.where(slot_of == 0, 0, jnp.where(slot_of == BPD - 1, CBY - 1, step_north))
    return jnp.stack([tile_east * CBX + step_east, tile_north * CBY + step_north]).astype(jnp.int32)


def draw_bound_body(key, part):
    index_all = jnp.arange(BTOT, dtype=jnp.int32)
    device_of = index_all // BPD
    slot_of = index_all % BPD
    tiles_north = N_GY * N_BODY
    tile_north = device_of % tiles_north
    beside = jnp.where(tile_north == tiles_north - 1, device_of - 1, device_of + 1)
    key_shift, key_local = jax.random.split(key)
    shifts = jax.random.randint(key_shift, (BTOT,), 0, 2)
    locals_drawn = jax.random.randint(key_local, (BTOT,), 0, BODY_DEV)
    labels = jnp.where(shifts == 1, beside, device_of) * BODY_DEV + locals_drawn
    labels = jnp.where(slot_of < BODY_DEV, device_of * BODY_DEV + slot_of, labels)
    return labels.astype(jnp.int32)


def draw_body_state(key, part):
    bodies = jnp.arange(NBODY, dtype=jnp.int32)
    home_device = bodies // BODY_DEV
    tiles_north = N_GY * N_BODY
    tile_east = (home_device // tiles_north).astype(jnp.float32)
    tile_north = (home_device % tiles_north).astype(jnp.float32)
    key_east, key_north, key_speed, key_spin = jax.random.split(key, 4)
    centre_east = (tile_east + jax.random.uniform(key_east, (NBODY,), jnp.float32)) * CBX
    centre_north = (tile_north + jax.random.uniform(key_north, (NBODY,), jnp.float32)) * CBY
    speeds = 0.3 * jax.random.normal(key_speed, (2, NBODY), jnp.float32)
    spin = 0.1 * jax.random.normal(key_spin, (NBODY,), jnp.float32)
    return jnp.concatenate([centre_east[None], centre_north[None], speeds, spin[None]], axis=0).astype(jnp.float32)


def shard_levels(rng, dims, cuts, least, high):
    def one(dim, parts):
        steps = jax.random.uniform(jax.random.fold_in(jax.random.fold_in(rng, 6), dim), (parts,), jnp.float32, least / len(cuts), high / len(cuts))
        return jnp.repeat(jnp.exp(steps), dims[dim] // parts).reshape((-1,) + (1,) * (len(dims) - dim - 1))

    level = one(*cuts[0])
    for cut in cuts[1:]:
        level = level * one(*cut)
    return level


def scatter_about(rng, shape, spread, bound, cuts=(), kind=jnp.bfloat16):
    factor_of = shard_levels(rng, shape, cuts, -0.22, 0.18) if cuts else 1.0
    result = jax.random.normal(rng, shape, jnp.float32) * spread * factor_of
    return jnp.minimum(jnp.maximum(result, -bound), bound).astype(kind)


def setup_inputs(seed: int = 0) -> dict:
    splits = jax.random.split(jax.random.key(seed), 10)
    return {
        "fluid_position": jnp.clip(1.0 * jax.random.uniform(splits[0], (NBX, 2, NBY, P_SIZE), jnp.float32) ** shard_levels(splits[0], (NBX, 2, NBY, P_SIZE), ((0, 8), (2, 32)), -0.2, 0.2), 0.0, 1.0),
        "fluid_velocity": scatter_about(splits[1], (NBX, 2, NBY, P_SIZE), 0.5, 3.0, ((0, 8), (2, 32)), jnp.float32),
        "fluid_volume": jnp.clip(jnp.exp(math.log(2.0) - 1.3862944 * jax.random.uniform(splits[2], (NBX, NBY, P_SIZE), jnp.float32) ** shard_levels(splits[2], (NBX, NBY, P_SIZE), ((0, 8), (1, 32)), -0.2, 0.2)), 0.5, 2.0),
        "bound_offset": jnp.clip(1.0 * jax.random.uniform(splits[3], (2, BTOT), jnp.float32) ** shard_levels(splits[3], (2, BTOT), ((1, 256),), -0.2, 0.2), 0.0, 1.0),
        "bound_cell": draw_bound_cell(jax.random.fold_in(splits[9], 71), 0),
        "bound_body": draw_bound_body(jax.random.fold_in(splits[9], 71), 0),
        "body_state": draw_body_state(jax.random.fold_in(splits[9], 71), 0),
        "mass_inverse": jnp.clip(jnp.exp(math.log(0.2) - 2.3025851 * jax.random.uniform(splits[7], (NBODY,), jnp.float32) ** shard_levels(splits[7], (NBODY,), ((0, 4),), -0.2, 0.2)), 0.02, 0.2),
        "inertia_inverse": jnp.clip(jnp.exp(math.log(0.02) - 2.30258502 * jax.random.uniform(splits[8], (NBODY,), jnp.float32) ** shard_levels(splits[8], (NBODY,), ((0, 4),), -0.2, 0.2)), 0.002, 0.02),
    }


gravity = 3.0
viscosity = 1.0
step_time = 0.05


def block_offsets(block_size):
    east_table = np.repeat(np.array([east_step - 1 for east_step in range(3) for north_step in range(3)], np.float32), block_size)
    north_table = np.repeat(np.array([north_step - 1 for east_step in range(3) for north_step in range(3)], np.float32), block_size)
    return jnp.asarray(east_table), jnp.asarray(north_table)


def gather_near(padded, tile_rows, tile_cols):
    pieces = [padded[east_step:east_step + tile_rows, :, north_step:north_step + tile_cols, :] for east_step in range(3) for north_step in range(3)]
    return jnp.concatenate(pieces, axis=-1)


def pair_terms(own_east, own_north, near_east, near_north):
    apart_east = own_east[..., :, None] - near_east[..., None, :]
    apart_north = own_north[..., :, None] - near_north[..., None, :]
    closeness = jnp.maximum(1.0 - apart_east * apart_east - apart_north * apart_north, 0.0)
    return apart_east, apart_north, closeness


def depth_row(own_state, nearby, offset_east, offset_north, block_size):
    apart_east, apart_north, closeness = pair_terms(own_state[0], own_state[1], nearby[0] + offset_east, nearby[1] + offset_north)
    return jnp.sum(nearby[4][:, None, :] * closeness * closeness * closeness, axis=-1) / block_size


def push_row(own_state, nearby, depths, depth_near, offset_east, offset_north, block_size):
    apart_east, apart_north, closeness = pair_terms(own_state[0], own_state[1], nearby[0] + offset_east, nearby[1] + offset_north)
    closer = closeness * closeness
    pressure = nearby[4][:, None, :] * (depths[:, :, None] + depth_near[:, None, :]) * (3.0 * closer)
    damping = nearby[4][:, None, :] * closer * closeness
    push_east = gravity * jnp.sum(pressure * apart_east, axis=-1) / block_size
    push_east = push_east + viscosity * jnp.sum(damping * (nearby[2][:, None, :] - own_state[2][:, :, None]), axis=-1) / block_size
    push_north = gravity * jnp.sum(pressure * apart_north, axis=-1) / block_size
    push_north = push_north + viscosity * jnp.sum(damping * (nearby[3][:, None, :] - own_state[3][:, :, None]), axis=-1) / block_size
    return jnp.stack([push_east, push_north])


def bound_force(near_group, depth_group, place_east, place_north, offset_east, offset_north, block_size):
    apart_east = place_east[:, None] - (near_group[:, 0] + offset_east)
    apart_north = place_north[:, None] - (near_group[:, 1] + offset_north)
    closeness = jnp.maximum(1.0 - apart_east * apart_east - apart_north * apart_north, 0.0)
    weights = near_group[:, 4] * depth_group * (6.0 * closeness * closeness)
    force_east = gravity * jnp.sum(weights * apart_east, axis=-1) / block_size
    force_north = gravity * jnp.sum(weights * apart_north, axis=-1) / block_size
    return jnp.stack([force_east, force_north])


def boundary_forces(nearby, depth_near, cell_east, cell_north, bound_offset, group_size, offset_east, offset_north, block_size):
    particle_count = bound_offset.shape[1]
    groups = particle_count // group_size

    def one_group(member):
        near_group = nearby[member[0], :, member[1]]
        depth_group = depth_near[member[0], member[1]]
        return bound_force(near_group, depth_group, member[2], member[3], offset_east, offset_north, block_size)

    stacked = lax.map(one_group, (cell_east.reshape(groups, group_size), cell_north.reshape(groups, group_size), bound_offset[0].reshape(groups, group_size), bound_offset[1].reshape(groups, group_size)))
    return jnp.transpose(stacked, (1, 0, 2)).reshape(2, particle_count)


def body_partials(forces, torques, labels, body_total):
    return jnp.stack([jax.ops.segment_sum(forces[0], labels, num_segments=body_total), jax.ops.segment_sum(forces[1], labels, num_segments=body_total), jax.ops.segment_sum(torques, labels, num_segments=body_total)])


def integrate(body_state, mass_inverse, inertia_inverse, body_sums):
    span_time = step_time * SUBSTEPS
    speed_east = body_state[2] + span_time * mass_inverse * body_sums[0]
    speed_north = body_state[3] + span_time * mass_inverse * body_sums[1]
    torques = body_sums[2] - (body_state[0] * body_sums[1] - body_state[1] * body_sums[0])
    spin = body_state[4] + span_time * inertia_inverse * torques
    return jnp.stack([speed_east, speed_north, spin])


def pad_blocks(values, cycle):
    return jnp.pad(values, ((cycle, cycle), (0, 0), (cycle, cycle), (0, 0)))


def reference(fluid_position, fluid_velocity, fluid_volume, bound_offset, bound_cell, bound_body, body_state, mass_inverse, inertia_inverse):
    tile_rows, tile_cols, block_size = fluid_position.shape[0], fluid_position.shape[2], fluid_position.shape[3]
    offset_east, offset_north = block_offsets(block_size)
    position, velocity = fluid_position, fluid_velocity
    volumes = fluid_volume[:, None]
    for substep in range(SUBSTEPS):
        particle_state = jnp.concatenate([position, velocity, volumes], axis=1)
        nearby = gather_near(pad_blocks(particle_state, 1), tile_rows, tile_cols)
        depths = lax.map(lambda member: depth_row(member[0], member[1], offset_east, offset_north, block_size), (particle_state, nearby))
        depth_near = gather_near(pad_blocks(depths[:, None], 1), tile_rows, tile_cols)[:, 0]
        pushes = lax.map(lambda member: push_row(member[0], member[1], member[2], member[3], offset_east, offset_north, block_size), (particle_state, nearby, depths, depth_near))
        last_near, last_depth_near, last_depths = nearby, depth_near, depths
        velocity = velocity + step_time * pushes
        position = position + step_time * velocity
    forces = boundary_forces(last_near, last_depth_near, bound_cell[0], bound_cell[1], bound_offset, BPD, offset_east, offset_north, block_size)
    place_east = bound_cell[0].astype(jnp.float32) + bound_offset[0]
    place_north = bound_cell[1].astype(jnp.float32) + bound_offset[1]
    torques = place_east * forces[1] - place_north * forces[0]
    body_sums = body_partials(forces, torques, bound_body, NBODY)
    motion = integrate(body_state, mass_inverse, inertia_inverse, body_sums)
    motion_table = jnp.concatenate([motion, body_state[0:2]], axis=0)
    picked = jnp.take(motion_table, bound_body, axis=1)
    bound_velocity = jnp.stack([picked[0] - picked[2] * (place_north - picked[4]), picked[1] + picked[2] * (place_east - picked[3])])
    return position, velocity, last_depths, motion, bound_velocity
```

```python
import jax
import jax.numpy as jnp
from jax import lax
from jax.experimental import pallas as pl
from jax.experimental.pallas import tpu as pltpu
from jax.sharding import PartitionSpec as P

SUBSTEPS = 3

gravity = 3.0
viscosity = 1.0
step_time = 0.05

ALONG_Y = ("gy", "body")
EVERY = ("gx", "gy", "body")
LANES = 128
FAR = 4096.0
F32 = jnp.float32
BF16 = jnp.bfloat16

STATE_ROWS = 8


def pieces(values):
    high = values.astype(BF16).astype(F32)
    rest = values - high
    middle = rest.astype(BF16).astype(F32)
    low = (rest - middle).astype(BF16).astype(F32)
    return high, middle, low


def near_rows(parts):
    high, middle, low = parts
    return [high, middle, low, high, middle, high]


def own_rows(parts):
    high, middle, low = parts
    return [high, high, high, middle, middle, low]


def row_iota(rows, lanes):
    return lax.broadcasted_iota(jnp.int32, (rows, lanes), 0)


def across(rows, pairs):
    dims = (((1,), (1,)), ((), ()))
    return lax.dot_general(rows, pairs, dims, preferred_element_type=F32)


class Tile:
    def __init__(self, rows, cols):
        self.rows, self.cols = rows, cols
        self.wide_rows, self.wide_cols = rows + 4, cols + 4
        self.ring_rows, self.ring_cols = rows + 2, cols + 2
        self.mask_rows = self.ring_rows + self.ring_cols
        self.depth = -(-(24 + self.mask_rows) // 16) * 16
        self.east_centre = float(self.wide_rows // 2)
        self.north_centre = float(self.wide_cols // 2)


def lane_block(ref_lanes):
    return lax.broadcasted_iota(jnp.int32, (1, ref_lanes), 1) // LANES


def substep_kernel(tile, with_push, with_bound, *refs):
    refs = list(refs)
    wide_ref = refs.pop(0)
    if with_bound:
        place_ref, cell_ref, slot_ref, shift_ref = (refs.pop(0) for _ in range(4))
    state_out = refs.pop(0) if with_push else None
    sums_out = refs.pop(0) if with_bound else None
    near_ref, own_ref, depth_ref, pair_ref, heavy_ref, drag_ref, sums_ref, back_ref, total_ref = refs
    rows, cols = tile.rows, tile.cols
    wide_lanes = tile.wide_cols * LANES
    ring_lanes = tile.ring_cols * LANES

    block_of = lane_block(wide_lanes)
    north_of = block_of.astype(F32) - tile.north_centre

    def place_of(r):
        state = wide_ref[r]
        east_shift = jnp.asarray(r, F32) - tile.east_centre
        return state[0:1] + east_shift, state[1:2] + north_of, state

    def feature_row(r, carry):
        east, north, state = place_of(r)
        size = state[4:5]
        reach = east * east + north * north
        near = jnp.concatenate([size, size * east, size * north, -(size * reach)], axis=0)
        near = jnp.concatenate(near_rows(pieces(near)), axis=0)
        extra = tile.depth - 24
        which = row_iota(extra, wide_lanes)
        is_row = which == r - 1
        is_col = which - tile.ring_rows == jnp.broadcast_to(block_of, (extra, wide_lanes)) - 1
        flags = jnp.where(is_row | is_col, jnp.broadcast_to(size, (extra, wide_lanes)), 0.0)
        near_ref[r] = jnp.concatenate([near, flags], axis=0).astype(BF16)
        return carry

    lax.fori_loop(0, tile.wide_rows, feature_row, 0)

    def own_features(east, north):
        reach = 1.0 - east * east - north * north
        own = jnp.concatenate([reach, 2.0 * east, 2.0 * north, jnp.ones_like(east)], axis=0)
        return jnp.concatenate(own_rows(pieces(own)), axis=0)

    def own_row(r, carry):
        east, north, state = place_of(r)
        own = own_features(east, north)
        own = jnp.concatenate([own, jnp.zeros((8, wide_lanes), F32)], axis=0)
        for c in range(tile.ring_cols):
            part = own[:, (c + 1) * LANES : (c + 2) * LANES]
            own_ref[r - 1, c] = part.T.astype(BF16)
        return carry

    lax.fori_loop(1, tile.ring_rows + 1, own_row, 0)

    def depth_block(r, c, keep):
        own = own_ref[r - 1, c - 1]
        total = jnp.zeros((LANES, LANES), F32)
        for e in range(3):
            start = pl.multiple_of((c - 1) * LANES, LANES)
            near = near_ref[r + e - 1, 0:32, pl.ds(start, 3 * LANES)]
            close = jnp.maximum(jnp.dot(own, near, preferred_element_type=F32), 0.0)
            second = close * close
            third = second * close
            for f in range(3):
                total = total + third[:, f * LANES : (f + 1) * LANES]
            if keep is not None:
                pair_ref[keep, :, pl.ds(e * 3 * LANES, 3 * LANES)] = second.astype(BF16)
                pair_ref[keep, :, pl.ds((9 + e * 3) * LANES, 3 * LANES)] = third.astype(BF16)
        depth = jnp.sum(total.T, axis=0, keepdims=True) * (1.0 / LANES)
        depth_ref[r - 1, 0:1, pl.ds(pl.multiple_of((c - 1) * LANES, LANES), LANES)] = depth

    def own_depth(k, carry):
        depth_block(k // cols + 2, k % cols + 2, k if with_push else None)
        return carry

    lax.fori_loop(0, rows * cols, own_depth, 0, unroll=8)

    def side_depth(k, carry):
        depth_block(1 + (rows + 1) * (k // tile.ring_cols), 1 + k % tile.ring_cols, None)
        return carry

    lax.fori_loop(0, 2 * tile.ring_cols, side_depth, 0, unroll=5)

    def end_depth(k, carry):
        depth_block(2 + k // 2, 1 + (cols + 1) * (k % 2), None)
        return carry

    lax.fori_loop(0, 2 * rows, end_depth, 0, unroll=4)

    def column_row(r, carry):
        east, north, state = place_of(r)
        inner = slice(LANES, LANES + ring_lanes)
        east, north, state = east[:, inner], north[:, inner], state[:, inner]
        size = state[4:5]
        heavy = size * depth_ref[r - 1, 0:1]
        blank = jnp.zeros((2, ring_lanes), F32)
        first = [size, heavy, size * east, size * north, heavy * east, heavy * north, blank]
        heavy_rows = jnp.concatenate(pieces(jnp.concatenate(first, axis=0)), axis=0)
        blank = jnp.zeros((24, ring_lanes), F32)
        heavy_all = jnp.concatenate([heavy_rows, blank], axis=0)
        if with_push:
            ones = jnp.ones((1, ring_lanes), F32)
            second = [state[2:4], ones, jnp.zeros((5, ring_lanes), F32)]
            drag_rows = jnp.concatenate(pieces(jnp.concatenate(second, axis=0)), axis=0)
            drag_all = jnp.concatenate([blank, drag_rows], axis=0)
        heavy_ref[r - 1] = heavy_all.astype(BF16)
        if with_push:
            drag_ref[r - 1] = drag_all.astype(BF16)
        return carry

    lax.fori_loop(1, tile.ring_rows + 1, column_row, 0)

    if with_bound:
        groups = place_ref.shape[1] // LANES
        cell = cell_ref[...]
        local = cell.astype(F32) - shift_ref[...]
        east = place_ref[0:1] + (local[0:1] + (2.0 - tile.east_centre))
        north = place_ref[1:2] + (local[1:2] + (2.0 - tile.north_centre))
        lanes = place_ref.shape[1]
        extra = tile.depth - 24
        which = row_iota(extra, lanes).astype(F32)
        apart_row = jnp.abs(which - (local[0:1] + 1.0))
        apart_col = jnp.abs(which - tile.ring_rows - (local[1:2] + 1.0))
        apart = jnp.where(which < tile.ring_rows - 0.5, apart_row, apart_col)
        apart = jnp.where(which < tile.mask_rows - 0.5, apart, 0.0)
        masks = jnp.where(apart > 1.5, -FAR, 0.0)
        bound = jnp.concatenate([own_features(east, north), masks], axis=0)
        for group in range(groups):
            back_ref[group] = bound[:, group * LANES : (group + 1) * LANES].T.astype(BF16)

        def bound_group(group, carry):
            own = back_ref[group]
            total = jnp.zeros((24, LANES), F32)
            for r in range(tile.ring_rows):
                near = near_ref[r + 1, :, LANES : LANES + ring_lanes]
                close = jnp.maximum(jnp.dot(own, near, preferred_element_type=F32), 0.0)
                second = close * close
                high = second.astype(BF16)
                low = (second - high.astype(F32)).astype(BF16)
                heavy = heavy_ref[r, 0:24]
                total = total + across(heavy, high) + across(heavy, low)
            merged = total[0:8] + total[8:16] + total[16:24]
            total_ref[:, pl.ds(pl.multiple_of(group * LANES, LANES), LANES)] = merged
            return carry

        lax.fori_loop(0, groups, bound_group, 0, unroll=2)
        merged = total_ref[...]
        factor = 6.0 * gravity / LANES
        force_east = factor * (east * merged[1:2] - merged[4:5])
        force_north = factor * (north * merged[1:2] - merged[5:6])
        cell_place = cell.astype(F32)
        torque = (cell_place[0:1] + place_ref[0:1]) * force_north
        torque = torque - (cell_place[1:2] + place_ref[1:2]) * force_east
        chosen = row_iota(8, lanes) == slot_ref[...]
        columns = []
        for values in (force_east, force_north, torque):
            picked = jnp.where(chosen, jnp.broadcast_to(values, (8, lanes)), 0.0)
            columns.append(jnp.sum(picked, axis=1, keepdims=True))
        lane = lax.broadcasted_iota(jnp.int32, (8, LANES), 1)
        result = jnp.where(lane == 0, columns[0], jnp.where(lane == 1, columns[1], columns[2]))
        sums_out[...] = result

    if with_push:

        def push_block(k, carry):
            r, c = k // cols, k % cols
            lanes = pl.ds(pl.multiple_of(c * LANES, LANES), 3 * LANES)
            near = [heavy_ref[r + e, :, lanes] for e in range(3)]
            near = near + [drag_ref[r + e, :, lanes] for e in range(3)]
            total = across(jnp.concatenate(near, axis=1), pair_ref[k])
            lanes = pl.ds(pl.multiple_of(c * LANES, LANES), LANES)
            sums_ref[r, 0:8, lanes] = total[0:8] + total[8:16] + total[16:24]
            sums_ref[r, 8:16, lanes] = total[24:32] + total[32:40] + total[40:48]
            return carry

        lax.fori_loop(0, rows * cols, push_block, 0, unroll=8)

        def update_row(r, carry):
            east, north, state = place_of(r + 2)
            inner = slice(2 * LANES, (2 + cols) * LANES)
            east, north, state = east[:, inner], north[:, inner], state[:, inner]
            sums = sums_ref[r]
            depth = depth_ref[r + 1, 0:1, LANES : (1 + cols) * LANES]
            speed_east, speed_north = state[2:3], state[3:4]
            heavy = depth * sums[0:1] + sums[1:2]
            push_east = heavy * east - depth * sums[2:3] - sums[4:5]
            push_north = heavy * north - depth * sums[3:4] - sums[5:6]
            drag_east = sums[8:9] - speed_east * sums[10:11]
            drag_north = sums[9:10] - speed_north * sums[10:11]
            scale = 3.0 * gravity / LANES
            thin = viscosity / LANES
            speed_east = speed_east + step_time * (scale * push_east + thin * drag_east)
            speed_north = speed_north + step_time * (scale * push_north + thin * drag_north)
            new = [
                state[0:1] + step_time * speed_east,
                state[1:2] + step_time * speed_north,
                speed_east,
                speed_north,
                state[4:5],
                depth,
                jnp.zeros((2, cols * LANES), F32),
            ]
            state_out[r] = jnp.concatenate(new, axis=0)
            return carry

        lax.fori_loop(0, rows, update_row, 0)


def run_substep(tile, wide, bound=None, with_push=True):
    rows, cols = tile.rows, tile.cols
    with_bound = bound is not None
    outs = []
    if with_push:
        outs.append(jax.ShapeDtypeStruct((rows, STATE_ROWS, cols * LANES), F32))
    if with_bound:
        outs.append(jax.ShapeDtypeStruct((8, LANES), F32))
    operands = [wide] + (list(bound) if with_bound else [])
    in_vmem = pl.BlockSpec(memory_space=pltpu.VMEM)
    bound_lanes = bound[0].shape[1] if with_bound else LANES
    ring = (tile.ring_rows, tile.ring_cols)

    def body(*refs):
        substep_kernel(tile, with_push, with_bound, *refs)

    return pl.pallas_call(
        body,
        out_shape=outs,
        in_specs=[in_vmem] * len(operands),
        out_specs=[in_vmem] * len(outs),
        scratch_shapes=[
            pltpu.VMEM((tile.wide_rows, tile.depth, tile.wide_cols * LANES), BF16),
            pltpu.VMEM(ring + (LANES, 32), BF16),
            pltpu.VMEM((tile.ring_rows, 8, tile.ring_cols * LANES), F32),
            pltpu.VMEM((rows * cols if with_push else 1, LANES, 18 * LANES), BF16),
            pltpu.VMEM((tile.ring_rows, 48, tile.ring_cols * LANES), BF16),
            pltpu.VMEM((tile.ring_rows, 48, tile.ring_cols * LANES), BF16),
            pltpu.VMEM((rows, 16, cols * LANES), F32),
            pltpu.VMEM((bound_lanes // LANES, LANES, tile.depth), BF16),
            pltpu.VMEM((8, bound_lanes), F32),
        ],
        compiler_params=pltpu.CompilerParams(vmem_limit_bytes=56 << 20),
        name="substep" + ("_push" if with_push else "") + ("_bound" if with_bound else ""),
    )(*operands)


def sent_both_ways(low_edge, high_edge, axis):
    count = lax.axis_size(axis)
    forward = [(i, i + 1) for i in range(count - 1)]
    backward = [(target, source) for source, target in forward]
    return lax.ppermute(high_edge, axis, forward), lax.ppermute(low_edge, axis, backward)


def with_halo(state):
    low, high = sent_both_ways(state[:2], state[-2:], "gx")
    state = jnp.concatenate([low, state, high], axis=0)
    side = 2 * LANES
    low, high = sent_both_ways(state[:, :, :side], state[:, :, -side:], ALONG_Y)
    return jnp.concatenate([low, state, high], axis=2)


def initial_state(position, velocity, volume):
    rows, _, cols, lanes = position.shape
    size = jnp.cbrt(volume)[:, None]
    blank = jnp.zeros((rows, STATE_ROWS - 5, cols, lanes), F32)
    state = jnp.concatenate([position, velocity, size, blank], axis=1)
    return state.reshape(rows, STATE_ROWS, cols * lanes)


def on_device(
    fluid_position,
    fluid_velocity,
    fluid_volume,
    bound_offset,
    bound_cell,
    bound_body,
    body_state,
    mass_inverse,
    inertia_inverse,
):
    rows, cols = fluid_position.shape[0], fluid_position.shape[2]
    tile = Tile(rows, cols)
    shard_bodies = body_state.shape[1]
    owners = lax.axis_size("body")
    devices = lax.axis_size(EVERY)
    tiles_north = lax.axis_size(ALONG_Y)
    body_total = shard_bodies * owners
    own_bodies = body_total // devices
    sharing = devices // owners
    me = lax.axis_index(EVERY)

    state = initial_state(fluid_position, fluid_velocity, fluid_volume)
    shift = jnp.stack([lax.axis_index("gx") * rows, lax.axis_index(ALONG_Y) * cols])
    shift = shift.astype(F32)[:, None]
    slot = bound_body - me * own_bodies
    slot = jnp.where(slot < 0, slot + 2 * own_bodies, slot)

    bodies = jnp.concatenate([body_state, mass_inverse[None], inertia_inverse[None]], axis=0)
    by_home = bodies.reshape(7, sharing, own_bodies)
    place = lax.broadcasted_iota(jnp.int32, (1, sharing, 1), 1) % tiles_north
    after = jnp.concatenate([by_home[:, 1:], by_home[:, -1:]], axis=1)
    before = jnp.concatenate([by_home[:, :1], by_home[:, :-1]], axis=1)
    beside = jnp.where(place == tiles_north - 1, before, after)
    params = jnp.concatenate([by_home, beside], axis=2)
    params = jnp.transpose(params, (1, 0, 2)).reshape(sharing, 7 * 2 * own_bodies)
    params = jnp.concatenate([params] * owners, axis=0)

    for _ in range(SUBSTEPS - 1):
        (state,) = run_substep(tile, with_halo(state))
    bound = (bound_offset, bound_cell, slot[None], shift)
    state, sums = run_substep(tile, with_halo(state), bound)

    partial = sums[:, :3].T.reshape(1, 6 * own_bodies)
    message = jnp.concatenate([jnp.broadcast_to(partial, (devices, 6 * own_bodies)), params], axis=1)
    received = lax.all_to_all(message, EVERY, 0, 0, tiled=True)
    partials = received[:, : 6 * own_bodies].reshape(devices, 3, 2 * own_bodies)
    partials = jnp.transpose(partials, (1, 0, 2))
    own_part, beside_part = partials[:, :, :own_bodies], partials[:, :, own_bodies:]
    place = lax.broadcasted_iota(jnp.int32, (1, devices, 1), 1) % tiles_north
    from_before = jnp.concatenate([beside_part[:, :1], beside_part[:, :-1]], axis=1)
    from_after = jnp.concatenate([beside_part[:, 1:], beside_part[:, -1:]], axis=1)
    totals = own_part + jnp.where(place > 0, from_before, 0.0)
    totals = totals + jnp.where(place == tiles_north - 2, from_after, 0.0)

    def integrate(state_of, mass_of, inertia_of, sums_of):
        span = step_time * SUBSTEPS
        east = state_of[2] + span * mass_of * sums_of[0]
        north = state_of[3] + span * mass_of * sums_of[1]
        torque = sums_of[2] - (state_of[0] * sums_of[1] - state_of[1] * sums_of[0])
        return jnp.stack([east, north, state_of[4] + span * inertia_of * torque])

    shard = lax.axis_index("body")
    shard_sums = lax.dynamic_slice_in_dim(totals, shard * sharing, sharing, axis=1)
    shard_sums = shard_sums.reshape(3, shard_bodies)
    motion = integrate(body_state, mass_inverse, inertia_inverse, shard_sums)

    tile_place = lax.axis_index(ALONG_Y)
    other = jnp.where(tile_place == tiles_north - 1, me - 1, me + 1)
    mine = lax.dynamic_slice_in_dim(totals, me, 1, axis=1)[:, 0]
    theirs = lax.dynamic_slice_in_dim(totals, other, 1, axis=1)[:, 0]
    local_sums = jnp.concatenate([mine, theirs], axis=1)
    local = lax.dynamic_slice_in_dim(received, me // sharing, 1, axis=0)[0, 6 * own_bodies :]
    local = local.reshape(7, 2 * own_bodies)
    local_motion = integrate(local[:5], local[5], local[6], local_sums)
    table = jnp.concatenate([local_motion, local[:2]], axis=0)
    chosen = slot[None, :, None] == jnp.arange(2 * own_bodies, dtype=jnp.int32)
    picked = jnp.sum(jnp.where(chosen, table[:, None, :], 0.0), axis=-1)
    place_east = bound_cell[0].astype(F32) + bound_offset[0]
    place_north = bound_cell[1].astype(F32) + bound_offset[1]
    bound_velocity = jnp.stack(
        [
            picked[0] - picked[2] * (place_north - picked[4]),
            picked[1] + picked[2] * (place_east - picked[3]),
        ]
    )
    shape = fluid_position.shape
    return (
        state[:, 0:2].reshape(shape),
        state[:, 2:4].reshape(shape),
        state[:, 5].reshape(fluid_volume.shape),
        motion,
        bound_velocity,
    )


def solution(mesh):
    return jax.shard_map(
        on_device,
        mesh=mesh,
        in_specs=(
            P("gx", None, ("gy", "body"), None),
            P("gx", None, ("gy", "body"), None),
            P("gx", ("gy", "body"), None),
            P(None, ("gx", "gy", "body")),
            P(None, ("gx", "gy", "body")),
            P(("gx", "gy", "body")),
            P(None, "body"),
            P("body"),
            P("body"),
        ),
        out_specs=(
            P("gx", None, ("gy", "body"), None),
            P("gx", None, ("gy", "body"), None),
            P("gx", ("gy", "body"), None),
            P(None, "body"),
            P(None, ("gx", "gy", "body")),
        ),
        check_vma=False,
    )
```

```python
import jax
import jax.numpy as jnp
from jax import lax
from jax.experimental import pallas as pl
from jax.experimental.pallas import tpu as pltpu
from jax.sharding import PartitionSpec as P

SUBSTEPS = 3

gravity = 3.0
viscosity = 1.0
step_time = 0.05

ALONG_Y = ("gy", "body")
EVERY = ("gx", "gy", "body")
LANES = 128
GROUP = 128
FAR = 4096.0
F32 = jnp.float32
BF16 = jnp.bfloat16

STATE_ROWS = 8


def pieces(values):
    high = values.astype(BF16).astype(F32)
    rest = values - high
    middle = rest.astype(BF16).astype(F32)
    low = (rest - middle).astype(BF16).astype(F32)
    return high, middle, low


def near_rows(parts):
    high, middle, low = parts
    return [high, middle, low, high, middle, high]


def own_rows(parts):
    high, middle, low = parts
    return [high, high, high, middle, middle, low]


def row_iota(rows, lanes):
    return lax.broadcasted_iota(jnp.int32, (rows, lanes), 0)


def across(rows, pairs):
    dims = (((1,), (1,)), ((), ()))
    return lax.dot_general(rows, pairs, dims, preferred_element_type=F32)


def lane_sums(values):
    return jnp.sum(values.T, axis=0, keepdims=True)


class Tile:
    def __init__(self, rows, cols):
        self.rows, self.cols = rows, cols
        self.wide_rows, self.wide_cols = rows + 4, cols + 4
        self.ring_rows, self.ring_cols = rows + 2, cols + 2
        self.mask_rows = self.ring_rows + self.ring_cols
        self.depth = -(-(24 + self.mask_rows) // 16) * 16
        self.east_centre = float(self.wide_rows // 2)
        self.north_centre = float(self.wide_cols // 2)


def lane_block(ref_lanes):
    return lax.broadcasted_iota(jnp.int32, (1, ref_lanes), 1) // LANES


def depth_half(tile, wide_ref, bound_refs, kept, scratch):
    with_bound = bound_refs is not None
    if with_bound:
        place_ref, cell_ref, slot_ref, shift_ref, sums_out, back_ref, total_ref, exact_ref = bound_refs
    depth_ref, pair_ref, heavy_ref, sums_ref = kept
    near_ref, own_ref, drag_ref = scratch
    rows, cols = tile.rows, tile.cols
    wide_lanes = tile.wide_cols * LANES
    ring_lanes = tile.ring_cols * LANES

    block_of = lane_block(wide_lanes)
    north_of = block_of.astype(F32) - tile.north_centre

    def place_of(r):
        state = wide_ref[r]
        east_shift = jnp.asarray(r, F32) - tile.east_centre
        return state[0:1] + east_shift, state[1:2] + north_of, state

    def feature_row(r, carry):
        east, north, state = place_of(r)
        size = state[4:5]
        reach = east * east + north * north
        near = jnp.concatenate([size, size * east, size * north, -(size * reach)], axis=0)
        near = jnp.concatenate(near_rows(pieces(near)), axis=0)
        extra = tile.depth - 24
        which = row_iota(extra, wide_lanes)
        is_row = which == r - 1
        is_col = which - tile.ring_rows == jnp.broadcast_to(block_of, (extra, wide_lanes)) - 1
        flags = jnp.where(is_row | is_col, jnp.broadcast_to(size, (extra, wide_lanes)), 0.0)
        near_ref[r] = jnp.concatenate([near, flags], axis=0).astype(BF16)
        return carry

    lax.fori_loop(0, tile.wide_rows, feature_row, 0, unroll=2)

    def own_features(east, north):
        reach = 1.0 - east * east - north * north
        own = jnp.concatenate([reach, 2.0 * east, 2.0 * north, jnp.ones_like(east)], axis=0)
        return jnp.concatenate(own_rows(pieces(own)), axis=0)

    def own_row(r, carry):
        east, north, state = place_of(r)
        own = own_features(east, north)
        own = jnp.concatenate([own, jnp.zeros((8, wide_lanes), F32)], axis=0)
        for c in range(tile.ring_cols):
            part = own[:, (c + 1) * LANES : (c + 2) * LANES]
            own_ref[r - 1, c] = part.T.astype(BF16)
        high, middle, _ = pieces(state[2:4, LANES : LANES + ring_lanes])
        ones = jnp.ones((1, ring_lanes), F32)
        blank = jnp.zeros((6, ring_lanes), F32)
        speeds = jnp.concatenate([high, ones, blank[:5], middle, blank], axis=0)
        drag_ref[r - 1] = speeds.astype(BF16)
        return carry

    lax.fori_loop(1, tile.ring_rows + 1, own_row, 0, unroll=2)

    def depth_block(r, c, keep):
        own = own_ref[r - 1, c - 1]
        lanes = pl.ds(pl.multiple_of((c - 1) * LANES, LANES), 3 * LANES)
        near = jnp.concatenate([near_ref[r + e - 1, 0:32, lanes] for e in range(3)], axis=1)
        all_close = jnp.maximum(jnp.dot(own, near, preferred_element_type=F32), 0.0)
        total = jnp.zeros((LANES, LANES), F32)
        thirds = []
        for block in range(9):
            close = all_close[:, block * LANES : (block + 1) * LANES]
            second = close * close
            third = second * close
            total = total + third
            if keep is not None:
                thirds.append(third.astype(BF16))
                high = second.astype(BF16)
                low = (second - high.astype(F32)).astype(BF16)
                pair_ref[keep, :, block * LANES : (block + 1) * LANES] = high
                pair_ref[keep, :, (9 + block) * LANES : (10 + block) * LANES] = low
        depth = lane_sums(total) * (1.0 / LANES)
        depth_ref[r - 1, 0:1, pl.ds(pl.multiple_of((c - 1) * LANES, LANES), LANES)] = depth
        if keep is not None:
            lanes = pl.ds(pl.multiple_of((c - 2) * LANES, LANES), 3 * LANES)
            speeds = jnp.concatenate([drag_ref[r + e - 2, :, lanes] for e in range(3)], axis=1)
            drag = across(speeds, jnp.concatenate(thirds, axis=1))
            lanes = pl.ds(pl.multiple_of((c - 2) * LANES, LANES), LANES)
            sums_ref[r - 2, 8:16, lanes] = drag[0:8] + drag[8:16]

    def own_depth(k, carry):
        depth_block(k // cols + 2, k % cols + 2, k)
        return carry

    lax.fori_loop(0, rows * cols, own_depth, 0, unroll=16)

    def side_depth(k, carry):
        depth_block(1 + (rows + 1) * (k // tile.ring_cols), 1 + k % tile.ring_cols, None)
        return carry

    lax.fori_loop(0, 2 * tile.ring_cols, side_depth, 0, unroll=10)

    def end_depth(k, carry):
        depth_block(2 + k // 2, 1 + (cols + 1) * (k % 2), None)
        return carry

    lax.fori_loop(0, 2 * rows, end_depth, 0, unroll=8)

    def column_row(r, carry):
        east, north, state = place_of(r)
        inner = slice(LANES, LANES + ring_lanes)
        east, north, state = east[:, inner], north[:, inner], state[:, inner]
        size = state[4:5]
        heavy = size * depth_ref[r - 1, 0:1]
        blank = jnp.zeros((2, ring_lanes), F32)
        first = [size, heavy, size * east, size * north, heavy * east, heavy * north, blank]
        first = jnp.concatenate(first, axis=0)
        if with_bound:
            exact_ref[r - 1] = first
        heavy_ref[r - 1] = jnp.concatenate(pieces(first), axis=0).astype(BF16)
        return carry

    lax.fori_loop(1, tile.ring_rows + 1, column_row, 0, unroll=2)

    if with_bound:
        groups = place_ref.shape[1] // GROUP
        cell = cell_ref[...]
        local = cell.astype(F32) - shift_ref[...]
        east = place_ref[0:1] + (local[0:1] + (2.0 - tile.east_centre))
        north = place_ref[1:2] + (local[1:2] + (2.0 - tile.north_centre))
        lanes = place_ref.shape[1]
        extra = tile.depth - 24
        which = row_iota(extra, lanes).astype(F32)
        apart_row = jnp.abs(which - (local[0:1] + 1.0))
        apart_col = jnp.abs(which - tile.ring_rows - (local[1:2] + 1.0))
        apart = jnp.where(which < tile.ring_rows - 0.5, apart_row, apart_col)
        apart = jnp.where(which < tile.mask_rows - 0.5, apart, 0.0)
        masks = jnp.where(apart > 1.5, -FAR, 0.0)
        bound = jnp.concatenate([own_features(east, north), masks], axis=0)
        for group in range(groups):
            back_ref[group] = bound[:, group * GROUP : (group + 1) * GROUP].T.astype(BF16)

        def bound_group(group, carry):
            own = back_ref[group]
            totals = [jnp.zeros((GROUP, LANES), F32) for _ in range(3)]
            for r in range(tile.ring_rows):
                near = near_ref[r + 1, :, LANES : LANES + ring_lanes]
                close = jnp.maximum(jnp.dot(own, near, preferred_element_type=F32), 0.0)
                for c in range(tile.ring_cols):
                    lanes = slice(c * LANES, (c + 1) * LANES)
                    second = close[:, lanes] * close[:, lanes]
                    for which, row in enumerate((1, 4, 5)):
                        weight = exact_ref[r, row : row + 1, lanes]
                        totals[which] = totals[which] + second * weight
            for which in range(3):
                total_ref[which, pl.ds(pl.multiple_of(group * GROUP, GROUP), GROUP)] = totals[which]
            return carry

        lax.fori_loop(0, groups, bound_group, 0)
        merged = []
        for which in range(3):
            parts = []
            for group in range(lanes // LANES):
                parts.append(lane_sums(total_ref[which, group * LANES : (group + 1) * LANES]))
            merged.append(jnp.concatenate(parts, axis=1))
        factor = 6.0 * gravity / LANES
        force_east = factor * (east * merged[0] - merged[1])
        force_north = factor * (north * merged[0] - merged[2])
        cell_place = cell.astype(F32)
        torque = (cell_place[0:1] + place_ref[0:1]) * force_north
        torque = torque - (cell_place[1:2] + place_ref[1:2]) * force_east
        chosen = row_iota(8, lanes) == slot_ref[...]
        columns = []
        for values in (force_east, force_north, torque):
            picked = jnp.where(chosen, jnp.broadcast_to(values, (8, lanes)), 0.0)
            columns.append(jnp.sum(picked, axis=1, keepdims=True))
        lane = lax.broadcasted_iota(jnp.int32, (8, LANES), 1)
        result = jnp.where(lane == 0, columns[0], jnp.where(lane == 1, columns[1], columns[2]))
        sums_out[...] = result


def push_half(tile, wide_ref, kept, state_out):
    depth_ref, pair_ref, heavy_ref, sums_ref = kept
    rows, cols = tile.rows, tile.cols
    north_of = lane_block(tile.wide_cols * LANES).astype(F32) - tile.north_centre

    def place_of(r):
        state = wide_ref[r]
        east_shift = jnp.asarray(r, F32) - tile.east_centre
        return state[0:1] + east_shift, state[1:2] + north_of, state

    def push_block(k, carry):
        r, c = k // cols, k % cols
        lanes = pl.ds(pl.multiple_of(c * LANES, LANES), 3 * LANES)
        near = [heavy_ref[r + e, :, lanes] for e in range(3)]
        total = across(jnp.concatenate(near + near, axis=1), pair_ref[k])
        lanes = pl.ds(pl.multiple_of(c * LANES, LANES), LANES)
        sums_ref[r, 0:8, lanes] = total[0:8] + total[8:16] + total[16:24]
        return carry

    lax.fori_loop(0, rows * cols, push_block, 0, unroll=8)

    def update_row(r, carry):
        east, north, state = place_of(r + 2)
        inner = slice(2 * LANES, (2 + cols) * LANES)
        east, north, state = east[:, inner], north[:, inner], state[:, inner]
        sums = sums_ref[r]
        depth = depth_ref[r + 1, 0:1, LANES : (1 + cols) * LANES]
        speed_east, speed_north = state[2:3], state[3:4]
        heavy = depth * sums[0:1] + sums[1:2]
        push_east = heavy * east - depth * sums[2:3] - sums[4:5]
        push_north = heavy * north - depth * sums[3:4] - sums[5:6]
        drag_east = sums[8:9] - speed_east * sums[10:11]
        drag_north = sums[9:10] - speed_north * sums[10:11]
        scale = 3.0 * gravity / LANES
        thin = viscosity / LANES
        speed_east = speed_east + step_time * (scale * push_east + thin * drag_east)
        speed_north = speed_north + step_time * (scale * push_north + thin * drag_north)
        new = [
            state[0:1] + step_time * speed_east,
            state[1:2] + step_time * speed_north,
            speed_east,
            speed_north,
            state[4:5],
            depth,
            jnp.zeros((2, cols * LANES), F32),
        ]
        state_out[r] = jnp.concatenate(new, axis=0)
        return carry

    lax.fori_loop(0, rows, update_row, 0, unroll=2)


def kept_shapes(tile):
    rows, cols = tile.rows, tile.cols
    return [
        ((tile.ring_rows, 8, tile.ring_cols * LANES), F32),
        ((rows * cols, LANES, 18 * LANES), BF16),
        ((tile.ring_rows, 24, tile.ring_cols * LANES), BF16),
        ((rows, 16, cols * LANES), F32),
    ]


def scratch_shapes(tile):
    return [
        ((tile.wide_rows, tile.depth, tile.wide_cols * LANES), BF16),
        ((tile.ring_rows, tile.ring_cols, LANES, 32), BF16),
        ((tile.ring_rows, 16, tile.ring_cols * LANES), BF16),
    ]


def in_vmem(shapes):
    return [pltpu.VMEM(shape, dtype) for shape, dtype in shapes]


VMEM_SPEC = pl.BlockSpec(memory_space=pltpu.VMEM)
LIMIT = 52 << 20


def run_substep(tile, wide):
    def body(wide_ref, state_out, *refs):
        kept, scratch = refs[:4], refs[4:]
        depth_half(tile, wide_ref, None, kept, scratch)
        push_half(tile, wide_ref, kept, state_out)

    return pl.pallas_call(
        body,
        out_shape=jax.ShapeDtypeStruct((tile.rows, STATE_ROWS, tile.cols * LANES), F32),
        in_specs=[VMEM_SPEC],
        out_specs=VMEM_SPEC,
        scratch_shapes=in_vmem(kept_shapes(tile) + scratch_shapes(tile)),
        compiler_params=pltpu.CompilerParams(vmem_limit_bytes=LIMIT),
        name="substep",
    )(wide)


def run_bound(tile, wide, bound):
    lanes = bound[0].shape[1]
    back = [
        ((lanes // GROUP, GROUP, tile.depth), BF16),
        ((3, lanes, LANES), F32),
        ((tile.ring_rows, 8, tile.ring_cols * LANES), F32),
    ]

    def body(wide_ref, place_ref, cell_ref, slot_ref, shift_ref, sums_out, *refs):
        kept, scratch, back_refs = refs[:4], refs[4:7], refs[7:]
        bound_refs = (place_ref, cell_ref, slot_ref, shift_ref, sums_out) + back_refs
        depth_half(tile, wide_ref, bound_refs, kept, scratch)

    sums = jax.ShapeDtypeStruct((8, LANES), F32)
    return pl.pallas_call(
        body,
        out_shape=[sums] + in_vmem(kept_shapes(tile)),
        in_specs=[VMEM_SPEC] * 5,
        out_specs=[VMEM_SPEC] * 5,
        scratch_shapes=in_vmem(scratch_shapes(tile) + back),
        compiler_params=pltpu.CompilerParams(vmem_limit_bytes=16 << 20),
        name="depth_bound",
    )(wide, *bound)


def run_push(tile, wide, kept):
    def body(wide_ref, depth_ref, pair_ref, heavy_ref, sums_ref, state_out):
        kept_refs = (depth_ref, pair_ref, heavy_ref, sums_ref)
        push_half(tile, wide_ref, kept_refs, state_out)

    return pl.pallas_call(
        body,
        out_shape=jax.ShapeDtypeStruct((tile.rows, STATE_ROWS, tile.cols * LANES), F32),
        in_specs=[VMEM_SPEC] * 5,
        out_specs=VMEM_SPEC,
        compiler_params=pltpu.CompilerParams(vmem_limit_bytes=16 << 20),
        cost_estimate=pl.CostEstimate(flops=8 * 10**9, bytes_accessed=2 * 10**7, transcendentals=0),
        name="push",
    )(wide, *kept)


def swapped_edges(low_edge, high_edge, axis):
    count = lax.axis_size(axis)
    odd = lax.axis_index(axis) % 2 == 1
    first = [(i, i ^ 1) for i in range(count)]
    second = [(i, ((i + 1) ^ 1) - 1) for i in range(1, count - 1)]
    to_first = jnp.where(odd, low_edge, high_edge)
    to_second = jnp.where(odd, high_edge, low_edge)
    from_second = lax.ppermute(to_second, axis, second)
    from_first = lax.ppermute(to_first, axis, first)
    low = jnp.where(odd, from_first, from_second)
    high = jnp.where(odd, from_second, from_first)
    return low, high


def with_halo(state):
    side = 2 * LANES
    low, high = swapped_edges(state[:, :, :side], state[:, :, -side:], ALONG_Y)
    state = jnp.concatenate([low, state, high], axis=2)
    low, high = swapped_edges(state[:2], state[-2:], "gx")
    return jnp.concatenate([low, state, high], axis=0)


def initial_state(position, velocity, volume):
    rows, _, cols, lanes = position.shape
    size = jnp.cbrt(volume)[:, None]
    blank = jnp.zeros((rows, STATE_ROWS - 5, cols, lanes), F32)
    state = jnp.concatenate([position, velocity, size, blank], axis=1)
    return state.reshape(rows, STATE_ROWS, cols * lanes)


def on_device(
    fluid_position,
    fluid_velocity,
    fluid_volume,
    bound_offset,
    bound_cell,
    bound_body,
    body_state,
    mass_inverse,
    inertia_inverse,
):
    rows, cols = fluid_position.shape[0], fluid_position.shape[2]
    tile = Tile(rows, cols)
    shard_bodies = body_state.shape[1]
    owners = lax.axis_size("body")
    devices = lax.axis_size(EVERY)
    tiles_north = lax.axis_size(ALONG_Y)
    body_total = shard_bodies * owners
    own_bodies = body_total // devices
    sharing = devices // owners
    me = lax.axis_index(EVERY)

    state = initial_state(fluid_position, fluid_velocity, fluid_volume)
    shift = jnp.stack([lax.axis_index("gx") * rows, lax.axis_index(ALONG_Y) * cols])
    shift = shift.astype(F32)[:, None]
    slot = bound_body - me * own_bodies
    slot = jnp.where(slot < 0, slot + 2 * own_bodies, slot)

    bodies = jnp.concatenate([body_state, mass_inverse[None], inertia_inverse[None]], axis=0)
    by_home = bodies.reshape(7, sharing, own_bodies)
    place = lax.broadcasted_iota(jnp.int32, (1, sharing, 1), 1) % tiles_north
    after = jnp.concatenate([by_home[:, 1:], by_home[:, -1:]], axis=1)
    before = jnp.concatenate([by_home[:, :1], by_home[:, :-1]], axis=1)
    beside = jnp.where(place == tiles_north - 1, before, after)
    params = jnp.concatenate([by_home, beside], axis=2)
    params = jnp.transpose(params, (1, 0, 2)).reshape(sharing, 7 * 2 * own_bodies)
    params = jnp.concatenate([params] * owners, axis=0)

    for _ in range(SUBSTEPS - 1):
        state = run_substep(tile, with_halo(state))
    bound = (bound_offset, bound_cell, slot[None], shift)
    wide = with_halo(state)
    sums, *kept = run_bound(tile, wide, bound)

    partial = sums[:, :3].T.reshape(1, 6 * own_bodies)
    message = jnp.concatenate([jnp.broadcast_to(partial, (devices, 6 * own_bodies)), params], axis=1)
    received = lax.all_to_all(message, EVERY, 0, 0, tiled=True)
    state = run_push(tile, wide, kept)
    partials = received[:, : 6 * own_bodies].reshape(devices, 3, 2 * own_bodies)
    partials = jnp.transpose(partials, (1, 0, 2))
    own_part, beside_part = partials[:, :, :own_bodies], partials[:, :, own_bodies:]
    place = lax.broadcasted_iota(jnp.int32, (1, devices, 1), 1) % tiles_north
    from_before = jnp.concatenate([beside_part[:, :1], beside_part[:, :-1]], axis=1)
    from_after = jnp.concatenate([beside_part[:, 1:], beside_part[:, -1:]], axis=1)
    totals = own_part + jnp.where(place > 0, from_before, 0.0)
    totals = totals + jnp.where(place == tiles_north - 2, from_after, 0.0)

    def integrate(state_of, mass_of, inertia_of, sums_of):
        span = step_time * SUBSTEPS
        east = state_of[2] + span * mass_of * sums_of[0]
        north = state_of[3] + span * mass_of * sums_of[1]
        torque = sums_of[2] - (state_of[0] * sums_of[1] - state_of[1] * sums_of[0])
        return jnp.stack([east, north, state_of[4] + span * inertia_of * torque])

    shard = lax.axis_index("body")
    shard_sums = lax.dynamic_slice_in_dim(totals, shard * sharing, sharing, axis=1)
    shard_sums = shard_sums.reshape(3, shard_bodies)
    motion = integrate(body_state, mass_inverse, inertia_inverse, shard_sums)

    tile_place = lax.axis_index(ALONG_Y)
    other = jnp.where(tile_place == tiles_north - 1, me - 1, me + 1)
    mine = lax.dynamic_slice_in_dim(totals, me, 1, axis=1)[:, 0]
    theirs = lax.dynamic_slice_in_dim(totals, other, 1, axis=1)[:, 0]
    local_sums = jnp.concatenate([mine, theirs], axis=1)
    local = lax.dynamic_slice_in_dim(received, me // sharing, 1, axis=0)[0, 6 * own_bodies :]
    local = local.reshape(7, 2 * own_bodies)
    local_motion = integrate(local[:5], local[5], local[6], local_sums)
    table = jnp.concatenate([local_motion, local[:2]], axis=0)
    chosen = slot[None, :, None] == jnp.arange(2 * own_bodies, dtype=jnp.int32)
    picked = jnp.sum(jnp.where(chosen, table[:, None, :], 0.0), axis=-1)
    place_east = bound_cell[0].astype(F32) + bound_offset[0]
    place_north = bound_cell[1].astype(F32) + bound_offset[1]
    bound_velocity = jnp.stack(
        [
            picked[0] - picked[2] * (place_north - picked[4]),
            picked[1] + picked[2] * (place_east - picked[3]),
        ]
    )
    shape = fluid_position.shape
    return (
        state[:, 0:2].reshape(shape),
        state[:, 2:4].reshape(shape),
        state[:, 5].reshape(fluid_volume.shape),
        motion,
        bound_velocity,
    )


def solution(mesh):
    return jax.shard_map(
        on_device,
        mesh=mesh,
        in_specs=(
            P("gx", None, ("gy", "body"), None),
            P("gx", None, ("gy", "body"), None),
            P("gx", ("gy", "body"), None),
            P(None, ("gx", "gy", "body")),
            P(None, ("gx", "gy", "body")),
            P(("gx", "gy", "body")),
            P(None, "body"),
            P("body"),
            P("body"),
        ),
        out_specs=(
            P("gx", None, ("gy", "body"), None),
            P("gx", None, ("gy", "body"), None),
            P("gx", ("gy", "body"), None),
            P(None, "body"),
            P(None, ("gx", "gy", "body")),
        ),
        check_vma=False,
    )
```

```python
import jax
import jax.numpy as jnp
from jax import lax
from jax.experimental import pallas as pl
from jax.experimental.pallas import tpu as pltpu
from jax.sharding import PartitionSpec as P

SUBSTEPS = 3

gravity = 3.0
viscosity = 1.0
step_time = 0.05

ALONG_Y = ("gy", "body")
EVERY = ("gx", "gy", "body")
LANES = 128
GROUP = 128
FAR = 4096.0
F32 = jnp.float32
BF16 = jnp.bfloat16

STATE_ROWS = 8


def pieces(values):
    high = values.astype(BF16).astype(F32)
    rest = values - high
    middle = rest.astype(BF16).astype(F32)
    low = (rest - middle).astype(BF16).astype(F32)
    return high, middle, low


def near_rows(parts):
    high, middle, low = parts
    return [high, middle, low, high, middle, high]


def own_rows(parts):
    high, middle, low = parts
    return [high, high, high, middle, middle, low]


def row_iota(rows, lanes):
    return lax.broadcasted_iota(jnp.int32, (rows, lanes), 0)


def across(rows, pairs):
    dims = (((1,), (1,)), ((), ()))
    return lax.dot_general(rows, pairs, dims, preferred_element_type=F32)


def lane_sums(values):
    return jnp.sum(values.T, axis=0, keepdims=True)


class Tile:
    def __init__(self, rows, cols):
        self.rows, self.cols = rows, cols
        self.wide_rows, self.wide_cols = rows + 4, cols + 4
        self.ring_rows, self.ring_cols = rows + 2, cols + 2
        self.mask_rows = self.ring_rows + self.ring_cols
        self.depth = -(-(24 + self.mask_rows) // 16) * 16
        self.east_centre = float(self.wide_rows // 2)
        self.north_centre = float(self.wide_cols // 2)


def lane_block(ref_lanes):
    return lax.broadcasted_iota(jnp.int32, (1, ref_lanes), 1) // LANES


def depth_half(tile, wide_ref, bound_refs, kept, scratch):
    with_bound = bound_refs is not None
    if with_bound:
        place_ref, cell_ref, slot_ref, shift_ref, sums_out, back_ref, total_ref, exact_ref = bound_refs
    depth_ref, pair_ref, heavy_ref, sums_ref = kept
    near_ref, own_ref, drag_ref = scratch
    rows, cols = tile.rows, tile.cols
    wide_lanes = tile.wide_cols * LANES
    ring_lanes = tile.ring_cols * LANES

    block_of = lane_block(wide_lanes)
    north_of = block_of.astype(F32) - tile.north_centre

    def place_of(r):
        state = wide_ref[r]
        east_shift = jnp.asarray(r, F32) - tile.east_centre
        return state[0:1] + east_shift, state[1:2] + north_of, state

    def feature_row(r, carry):
        east, north, state = place_of(r)
        size = state[4:5]
        reach = east * east + north * north
        near = jnp.concatenate([size, size * east, size * north, -(size * reach)], axis=0)
        near = jnp.concatenate(near_rows(pieces(near)), axis=0)
        extra = tile.depth - 24
        which = row_iota(extra, wide_lanes)
        is_row = which == r - 1
        is_col = which - tile.ring_rows == jnp.broadcast_to(block_of, (extra, wide_lanes)) - 1
        flags = jnp.where(is_row | is_col, jnp.broadcast_to(size, (extra, wide_lanes)), 0.0)
        near_ref[r] = jnp.concatenate([near, flags], axis=0).astype(BF16)
        return carry

    lax.fori_loop(0, tile.wide_rows, feature_row, 0, unroll=2)

    def own_features(east, north):
        reach = 1.0 - east * east - north * north
        own = jnp.concatenate([reach, 2.0 * east, 2.0 * north, jnp.ones_like(east)], axis=0)
        return jnp.concatenate(own_rows(pieces(own)), axis=0)

    def own_row(r, carry):
        east, north, state = place_of(r)
        own = own_features(east, north)
        own = jnp.concatenate([own, jnp.zeros((8, wide_lanes), F32)], axis=0)
        for c in range(tile.ring_cols):
            part = own[:, (c + 1) * LANES : (c + 2) * LANES]
            own_ref[r - 1, c] = part.T.astype(BF16)
        high, middle, _ = pieces(state[2:4, LANES : LANES + ring_lanes])
        ones = jnp.ones((1, ring_lanes), F32)
        blank = jnp.zeros((6, ring_lanes), F32)
        speeds = jnp.concatenate([high, ones, blank[:5], middle, blank], axis=0)
        drag_ref[r - 1] = speeds.astype(BF16)
        return carry

    lax.fori_loop(1, tile.ring_rows + 1, own_row, 0, unroll=2)

    def depth_block(r, c, keep):
        own = own_ref[r - 1, c - 1]
        lanes = pl.ds(pl.multiple_of((c - 1) * LANES, LANES), 3 * LANES)
        near = jnp.concatenate([near_ref[r + e - 1, 0:32, lanes] for e in range(3)], axis=1)
        all_close = jnp.maximum(jnp.dot(own, near, preferred_element_type=F32), 0.0)
        total = jnp.zeros((LANES, LANES), F32)
        thirds = []
        for block in range(9):
            close = all_close[:, block * LANES : (block + 1) * LANES]
            second = close * close
            third = second * close
            total = total + third
            if keep is not None:
                thirds.append(third.astype(BF16))
                high = second.astype(BF16)
                low = (second - high.astype(F32)).astype(BF16)
                pair_ref[keep, :, block * LANES : (block + 1) * LANES] = high
                pair_ref[keep, :, (9 + block) * LANES : (10 + block) * LANES] = low
        depth = lane_sums(total) * (1.0 / LANES)
        depth_ref[r - 1, 0:1, pl.ds(pl.multiple_of((c - 1) * LANES, LANES), LANES)] = depth
        if keep is not None:
            lanes = pl.ds(pl.multiple_of((c - 2) * LANES, LANES), 3 * LANES)
            speeds = jnp.concatenate([drag_ref[r + e - 2, :, lanes] for e in range(3)], axis=1)
            drag = across(speeds, jnp.concatenate(thirds, axis=1))
            lanes = pl.ds(pl.multiple_of((c - 2) * LANES, LANES), LANES)
            sums_ref[r - 2, 8:16, lanes] = drag[0:8] + drag[8:16]

    def own_depth(k, carry):
        depth_block(k // cols + 2, k % cols + 2, k)
        return carry

    lax.fori_loop(0, rows * cols, own_depth, 0, unroll=16)

    def side_depth(k, carry):
        depth_block(1 + (rows + 1) * (k // tile.ring_cols), 1 + k % tile.ring_cols, None)
        return carry

    lax.fori_loop(0, 2 * tile.ring_cols, side_depth, 0, unroll=10)

    def end_depth(k, carry):
        depth_block(2 + k // 2, 1 + (cols + 1) * (k % 2), None)
        return carry

    lax.fori_loop(0, 2 * rows, end_depth, 0, unroll=8)

    def column_row(r, carry):
        east, north, state = place_of(r)
        inner = slice(LANES, LANES + ring_lanes)
        east, north, state = east[:, inner], north[:, inner], state[:, inner]
        size = state[4:5]
        heavy = size * depth_ref[r - 1, 0:1]
        blank = jnp.zeros((2, ring_lanes), F32)
        first = [size, heavy, size * east, size * north, heavy * east, heavy * north, blank]
        first = jnp.concatenate(first, axis=0)
        if with_bound:
            exact_ref[r - 1] = first
        heavy_ref[r - 1] = jnp.concatenate(pieces(first), axis=0).astype(BF16)
        return carry

    lax.fori_loop(1, tile.ring_rows + 1, column_row, 0, unroll=2)

    if with_bound:
        groups = place_ref.shape[1] // GROUP
        cell = cell_ref[...]
        local = cell.astype(F32) - shift_ref[...]
        east = place_ref[0:1] + (local[0:1] + (2.0 - tile.east_centre))
        north = place_ref[1:2] + (local[1:2] + (2.0 - tile.north_centre))
        lanes = place_ref.shape[1]
        extra = tile.depth - 24
        which = row_iota(extra, lanes).astype(F32)
        apart_row = jnp.abs(which - (local[0:1] + 1.0))
        apart_col = jnp.abs(which - tile.ring_rows - (local[1:2] + 1.0))
        apart = jnp.where(which < tile.ring_rows - 0.5, apart_row, apart_col)
        apart = jnp.where(which < tile.mask_rows - 0.5, apart, 0.0)
        masks = jnp.where(apart > 1.5, -FAR, 0.0)
        bound = jnp.concatenate([own_features(east, north), masks], axis=0)
        for group in range(groups):
            back_ref[group] = bound[:, group * GROUP : (group + 1) * GROUP].T.astype(BF16)

        def bound_group(group, carry):
            own = back_ref[group]
            totals = [jnp.zeros((GROUP, LANES), F32) for _ in range(3)]
            for r in range(tile.ring_rows):
                near = near_ref[r + 1, :, LANES : LANES + ring_lanes]
                close = jnp.maximum(jnp.dot(own, near, preferred_element_type=F32), 0.0)
                for c in range(tile.ring_cols):
                    lanes = slice(c * LANES, (c + 1) * LANES)
                    second = close[:, lanes] * close[:, lanes]
                    for which, row in enumerate((1, 4, 5)):
                        weight = exact_ref[r, row : row + 1, lanes]
                        totals[which] = totals[which] + second * weight
            for which in range(3):
                total_ref[which, pl.ds(pl.multiple_of(group * GROUP, GROUP), GROUP)] = totals[which]
            return carry

        lax.fori_loop(0, groups, bound_group, 0)
        merged = []
        for which in range(3):
            parts = []
            for group in range(lanes // LANES):
                parts.append(lane_sums(total_ref[which, group * LANES : (group + 1) * LANES]))
            merged.append(jnp.concatenate(parts, axis=1))
        factor = 6.0 * gravity / LANES
        force_east = factor * (east * merged[0] - merged[1])
        force_north = factor * (north * merged[0] - merged[2])
        cell_place = cell.astype(F32)
        torque = (cell_place[0:1] + place_ref[0:1]) * force_north
        torque = torque - (cell_place[1:2] + place_ref[1:2]) * force_east
        chosen = row_iota(8, lanes) == slot_ref[...]
        columns = []
        for values in (force_east, force_north, torque):
            picked = jnp.where(chosen, jnp.broadcast_to(values, (8, lanes)), 0.0)
            columns.append(jnp.sum(picked, axis=1, keepdims=True))
        lane = lax.broadcasted_iota(jnp.int32, (8, LANES), 1)
        result = jnp.where(lane == 0, columns[0], jnp.where(lane == 1, columns[1], columns[2]))
        sums_out[...] = result


def push_half(tile, wide_ref, kept, state_out, final_out=None):
    depth_ref, pair_ref, heavy_ref, sums_ref = kept
    rows, cols = tile.rows, tile.cols
    north_of = lane_block(tile.wide_cols * LANES).astype(F32) - tile.north_centre

    def place_of(r):
        state = wide_ref[r]
        east_shift = jnp.asarray(r, F32) - tile.east_centre
        return state[0:1] + east_shift, state[1:2] + north_of, state

    def push_block(k, carry):
        r, c = k // cols, k % cols
        lanes = pl.ds(pl.multiple_of(c * LANES, LANES), 3 * LANES)
        near = [heavy_ref[r + e, :, lanes] for e in range(3)]
        total = across(jnp.concatenate(near + near, axis=1), pair_ref[k])
        lanes = pl.ds(pl.multiple_of(c * LANES, LANES), LANES)
        sums_ref[r, 0:8, lanes] = total[0:8] + total[8:16] + total[16:24]
        return carry

    lax.fori_loop(0, rows * cols, push_block, 0, unroll=8)

    def update_row(r, carry):
        east, north, state = place_of(r + 2)
        inner = slice(2 * LANES, (2 + cols) * LANES)
        east, north, state = east[:, inner], north[:, inner], state[:, inner]
        sums = sums_ref[r]
        depth = depth_ref[r + 1, 0:1, LANES : (1 + cols) * LANES]
        speed_east, speed_north = state[2:3], state[3:4]
        heavy = depth * sums[0:1] + sums[1:2]
        push_east = heavy * east - depth * sums[2:3] - sums[4:5]
        push_north = heavy * north - depth * sums[3:4] - sums[5:6]
        drag_east = sums[8:9] - speed_east * sums[10:11]
        drag_north = sums[9:10] - speed_north * sums[10:11]
        scale = 3.0 * gravity / LANES
        thin = viscosity / LANES
        speed_east = speed_east + step_time * (scale * push_east + thin * drag_east)
        speed_north = speed_north + step_time * (scale * push_north + thin * drag_north)
        east = state[0:1] + step_time * speed_east
        north = state[1:2] + step_time * speed_north
        if state_out is not None:
            blank = jnp.zeros((STATE_ROWS - 5, cols * LANES), F32)
            new = [east, north, speed_east, speed_north, state[4:5], blank]
            state_out[r] = jnp.concatenate(new, axis=0)
        else:
            position_out, velocity_out, depth_out = final_out
            for c in range(cols):
                lanes = slice(c * LANES, (c + 1) * LANES)
                position_out[r, 0, c : c + 1] = east[:, lanes]
                position_out[r, 1, c : c + 1] = north[:, lanes]
                velocity_out[r, 0, c : c + 1] = speed_east[:, lanes]
                velocity_out[r, 1, c : c + 1] = speed_north[:, lanes]
                depth_out[r, c : c + 1] = depth[:, lanes]
        return carry

    lax.fori_loop(0, rows, update_row, 0, unroll=2)


def kept_shapes(tile):
    rows, cols = tile.rows, tile.cols
    return [
        ((tile.ring_rows, 8, tile.ring_cols * LANES), F32),
        ((rows * cols, LANES, 18 * LANES), BF16),
        ((tile.ring_rows, 24, tile.ring_cols * LANES), BF16),
        ((rows, 16, cols * LANES), F32),
    ]


def scratch_shapes(tile):
    return [
        ((tile.wide_rows, tile.depth, tile.wide_cols * LANES), BF16),
        ((tile.ring_rows, tile.ring_cols, LANES, 32), BF16),
        ((tile.ring_rows, 16, tile.ring_cols * LANES), BF16),
    ]


def in_vmem(shapes):
    return [pltpu.VMEM(shape, dtype) for shape, dtype in shapes]


VMEM_SPEC = pl.BlockSpec(memory_space=pltpu.VMEM)
LIMIT = 52 << 20


def run_substep(tile, wide):
    def body(wide_ref, state_out, *refs):
        kept, scratch = refs[:4], refs[4:]
        depth_half(tile, wide_ref, None, kept, scratch)
        push_half(tile, wide_ref, kept, state_out)

    return pl.pallas_call(
        body,
        out_shape=jax.ShapeDtypeStruct((tile.rows, STATE_ROWS, tile.cols * LANES), F32),
        in_specs=[VMEM_SPEC],
        out_specs=VMEM_SPEC,
        scratch_shapes=in_vmem(kept_shapes(tile) + scratch_shapes(tile)),
        compiler_params=pltpu.CompilerParams(vmem_limit_bytes=LIMIT),
        name="substep",
    )(wide)


def run_bound(tile, wide, bound):
    lanes = bound[0].shape[1]
    back = [
        ((lanes // GROUP, GROUP, tile.depth), BF16),
        ((3, lanes, LANES), F32),
        ((tile.ring_rows, 8, tile.ring_cols * LANES), F32),
    ]

    def body(wide_ref, place_ref, cell_ref, slot_ref, shift_ref, sums_out, *refs):
        kept, scratch, back_refs = refs[:4], refs[4:7], refs[7:]
        bound_refs = (place_ref, cell_ref, slot_ref, shift_ref, sums_out) + back_refs
        depth_half(tile, wide_ref, bound_refs, kept, scratch)

    sums = jax.ShapeDtypeStruct((8, LANES), F32)
    return pl.pallas_call(
        body,
        out_shape=[sums] + in_vmem(kept_shapes(tile)),
        in_specs=[VMEM_SPEC] * 5,
        out_specs=[VMEM_SPEC] * 5,
        scratch_shapes=in_vmem(scratch_shapes(tile) + back),
        compiler_params=pltpu.CompilerParams(vmem_limit_bytes=16 << 20),
        name="depth_bound",
    )(wide, *bound)


def run_push(tile, wide, kept):
    rows, cols = tile.rows, tile.cols
    pair = jax.ShapeDtypeStruct((rows, 2, cols, LANES), F32)

    def body(wide_ref, depth_ref, pair_ref, heavy_ref, sums_ref, *final_out):
        kept_refs = (depth_ref, pair_ref, heavy_ref, sums_ref)
        push_half(tile, wide_ref, kept_refs, None, final_out)

    return pl.pallas_call(
        body,
        out_shape=[pair, pair, jax.ShapeDtypeStruct((rows, cols, LANES), F32)],
        in_specs=[VMEM_SPEC] * 5,
        out_specs=[VMEM_SPEC] * 3,
        compiler_params=pltpu.CompilerParams(vmem_limit_bytes=16 << 20),
        cost_estimate=pl.CostEstimate(flops=8 * 10**9, bytes_accessed=2 * 10**7, transcendentals=0),
        name="push",
    )(wide, *kept)


def swapped_edges(low_edge, high_edge, axis):
    count = lax.axis_size(axis)
    odd = lax.axis_index(axis) % 2 == 1
    first = [(i, i ^ 1) for i in range(count)]
    second = [(i, ((i + 1) ^ 1) - 1) for i in range(1, count - 1)]
    to_first = jnp.where(odd, low_edge, high_edge)
    to_second = jnp.where(odd, high_edge, low_edge)
    from_second = lax.ppermute(to_second, axis, second)
    from_first = lax.ppermute(to_first, axis, first)
    low = jnp.where(odd, from_first, from_second)
    high = jnp.where(odd, from_second, from_first)
    return low, high


def with_halo(state):
    side = 2 * LANES
    low, high = swapped_edges(state[:, :, :side], state[:, :, -side:], ALONG_Y)
    state = jnp.concatenate([low, state, high], axis=2)
    low, high = swapped_edges(state[:2], state[-2:], "gx")
    return jnp.concatenate([low, state, high], axis=0)


def initial_state(position, velocity, volume):
    rows, _, cols, lanes = position.shape

    def body(position_ref, velocity_ref, volume_ref, state_out):
        blank = jnp.zeros((STATE_ROWS - 5, LANES), F32)
        for r in range(rows):
            volumes = volume_ref[r]
            size = jnp.exp(jnp.log(volumes) * (1.0 / 3.0))
            square = size * size
            size = size - (square * size - volumes) / (3.0 * square)
            for c in range(cols):
                row = slice(c, c + 1)
                new = [
                    position_ref[r, 0, row],
                    position_ref[r, 1, row],
                    velocity_ref[r, 0, row],
                    velocity_ref[r, 1, row],
                    size[row],
                    blank,
                ]
                state_out[r, :, c * LANES : (c + 1) * LANES] = jnp.concatenate(new, axis=0)

    return pl.pallas_call(
        body,
        out_shape=jax.ShapeDtypeStruct((rows, STATE_ROWS, cols * lanes), F32),
        in_specs=[VMEM_SPEC] * 3,
        out_specs=VMEM_SPEC,
        name="initial",
    )(position, velocity, volume)


def on_device(
    fluid_position,
    fluid_velocity,
    fluid_volume,
    bound_offset,
    bound_cell,
    bound_body,
    body_state,
    mass_inverse,
    inertia_inverse,
):
    rows, cols = fluid_position.shape[0], fluid_position.shape[2]
    tile = Tile(rows, cols)
    shard_bodies = body_state.shape[1]
    owners = lax.axis_size("body")
    devices = lax.axis_size(EVERY)
    tiles_north = lax.axis_size(ALONG_Y)
    body_total = shard_bodies * owners
    own_bodies = body_total // devices
    sharing = devices // owners
    me = lax.axis_index(EVERY)

    state = initial_state(fluid_position, fluid_velocity, fluid_volume)
    shift = jnp.stack([lax.axis_index("gx") * rows, lax.axis_index(ALONG_Y) * cols])
    shift = shift.astype(F32)[:, None]
    slot = bound_body - me * own_bodies
    slot = jnp.where(slot < 0, slot + 2 * own_bodies, slot)

    bodies = jnp.concatenate([body_state, mass_inverse[None], inertia_inverse[None]], axis=0)
    by_home = bodies.reshape(7, sharing, own_bodies)
    place = lax.broadcasted_iota(jnp.int32, (1, sharing, 1), 1) % tiles_north
    after = jnp.concatenate([by_home[:, 1:], by_home[:, -1:]], axis=1)
    before = jnp.concatenate([by_home[:, :1], by_home[:, :-1]], axis=1)
    beside = jnp.where(place == tiles_north - 1, before, after)
    params = jnp.concatenate([by_home, beside], axis=2)
    params = jnp.transpose(params, (1, 0, 2)).reshape(sharing, 7 * 2 * own_bodies)
    params = jnp.concatenate([params] * owners, axis=0)

    for _ in range(SUBSTEPS - 1):
        state = run_substep(tile, with_halo(state))
    bound = (bound_offset, bound_cell, slot[None], shift)
    wide = with_halo(state)
    sums, *kept = run_bound(tile, wide, bound)

    partial = sums[:, :3].T.reshape(1, 6 * own_bodies)
    message = jnp.concatenate([jnp.broadcast_to(partial, (devices, 6 * own_bodies)), params], axis=1)
    received = lax.all_to_all(message, EVERY, 0, 0, tiled=True)
    position, velocity, depth = run_push(tile, wide, kept)
    partials = received[:, : 6 * own_bodies].reshape(devices, 3, 2 * own_bodies)
    partials = jnp.transpose(partials, (1, 0, 2))
    own_part, beside_part = partials[:, :, :own_bodies], partials[:, :, own_bodies:]
    place = lax.broadcasted_iota(jnp.int32, (1, devices, 1), 1) % tiles_north
    from_before = jnp.concatenate([beside_part[:, :1], beside_part[:, :-1]], axis=1)
    from_after = jnp.concatenate([beside_part[:, 1:], beside_part[:, -1:]], axis=1)
    totals = own_part + jnp.where(place > 0, from_before, 0.0)
    totals = totals + jnp.where(place == tiles_north - 2, from_after, 0.0)

    def integrate(state_of, mass_of, inertia_of, sums_of):
        span = step_time * SUBSTEPS
        east = state_of[2] + span * mass_of * sums_of[0]
        north = state_of[3] + span * mass_of * sums_of[1]
        torque = sums_of[2] - (state_of[0] * sums_of[1] - state_of[1] * sums_of[0])
        return jnp.stack([east, north, state_of[4] + span * inertia_of * torque])

    shard = lax.axis_index("body")
    shard_sums = lax.dynamic_slice_in_dim(totals, shard * sharing, sharing, axis=1)
    shard_sums = shard_sums.reshape(3, shard_bodies)
    motion = integrate(body_state, mass_inverse, inertia_inverse, shard_sums)

    tile_place = lax.axis_index(ALONG_Y)
    other = jnp.where(tile_place == tiles_north - 1, me - 1, me + 1)
    mine = lax.dynamic_slice_in_dim(totals, me, 1, axis=1)[:, 0]
    theirs = lax.dynamic_slice_in_dim(totals, other, 1, axis=1)[:, 0]
    local_sums = jnp.concatenate([mine, theirs], axis=1)
    local = lax.dynamic_slice_in_dim(received, me // sharing, 1, axis=0)[0, 6 * own_bodies :]
    local = local.reshape(7, 2 * own_bodies)
    local_motion = integrate(local[:5], local[5], local[6], local_sums)
    table = jnp.concatenate([local_motion, local[:2]], axis=0)
    chosen = slot[None, :, None] == jnp.arange(2 * own_bodies, dtype=jnp.int32)
    picked = jnp.sum(jnp.where(chosen, table[:, None, :], 0.0), axis=-1)
    place_east = bound_cell[0].astype(F32) + bound_offset[0]
    place_north = bound_cell[1].astype(F32) + bound_offset[1]
    bound_velocity = jnp.stack(
        [
            picked[0] - picked[2] * (place_north - picked[4]),
            picked[1] + picked[2] * (place_east - picked[3]),
        ]
    )
    return position, velocity, depth, motion, bound_velocity


def solution(mesh):
    return jax.shard_map(
        on_device,
        mesh=mesh,
        in_specs=(
            P("gx", None, ("gy", "body"), None),
            P("gx", None, ("gy", "body"), None),
            P("gx", ("gy", "body"), None),
            P(None, ("gx", "gy", "body")),
            P(None, ("gx", "gy", "body")),
            P(("gx", "gy", "body")),
            P(None, "body"),
            P("body"),
            P("body"),
        ),
        out_specs=(
            P("gx", None, ("gy", "body"), None),
            P("gx", None, ("gy", "body"), None),
            P("gx", ("gy", "body"), None),
            P(None, "body"),
            P(None, ("gx", "gy", "body")),
        ),
        check_vma=False,
    )
```

```python
import jax
import jax.numpy as jnp
from jax import lax
from jax.experimental import pallas as pl
from jax.experimental.pallas import tpu as pltpu
from jax.sharding import PartitionSpec as P

SUBSTEPS = 3

gravity = 3.0
viscosity = 1.0
step_time = 0.05

ALONG_Y = ("gy", "body")
EVERY = ("gx", "gy", "body")
LANES = 128
GROUP = 128
FAR = 4096.0
F32 = jnp.float32
BF16 = jnp.bfloat16

STATE_ROWS = 8


def pieces(values):
    high = values.astype(BF16).astype(F32)
    rest = values - high
    middle = rest.astype(BF16).astype(F32)
    low = (rest - middle).astype(BF16).astype(F32)
    return high, middle, low


def near_rows(parts):
    high, middle, low = parts
    return [high, middle, low, high, middle, high]


def own_rows(parts):
    high, middle, low = parts
    return [high, high, high, middle, middle, low]


def row_iota(rows, lanes):
    return lax.broadcasted_iota(jnp.int32, (rows, lanes), 0)


def across(rows, pairs):
    dims = (((1,), (1,)), ((), ()))
    return lax.dot_general(rows, pairs, dims, preferred_element_type=F32)


def lane_sums(values):
    return jnp.sum(values.T, axis=0, keepdims=True)


class Tile:
    def __init__(self, rows, cols):
        self.rows, self.cols = rows, cols
        self.wide_rows, self.wide_cols = rows + 4, cols + 4
        self.ring_rows, self.ring_cols = rows + 2, cols + 2
        self.mask_rows = self.ring_rows + self.ring_cols
        self.depth = -(-(24 + self.mask_rows) // 16) * 16
        self.east_centre = float(self.wide_rows // 2)
        self.north_centre = float(self.wide_cols // 2)


def lane_block(ref_lanes):
    return lax.broadcasted_iota(jnp.int32, (1, ref_lanes), 1) // LANES


def depth_half(tile, wide_ref, bound_refs, kept, scratch):
    with_bound = bound_refs is not None
    if with_bound:
        (place_ref, cell_ref, slot_ref, shift_ref, sums_out, back_ref, total_ref, exact_ref) = bound_refs[:8]
        place_all, cell_all, pair_all, copies = bound_refs[8:]
        place_copy = pltpu.make_async_copy(place_all, place_ref, copies.at[0])
        cell_copy = pltpu.make_async_copy(cell_all, cell_ref, copies.at[1])
        place_copy.start()
        cell_copy.start()
    depth_ref, pair_ref, heavy_ref, sums_ref = kept
    near_ref, own_ref, drag_ref = scratch
    rows, cols = tile.rows, tile.cols
    wide_lanes = tile.wide_cols * LANES
    ring_lanes = tile.ring_cols * LANES

    block_of = lane_block(wide_lanes)
    north_of = block_of.astype(F32) - tile.north_centre

    def place_of(r):
        state = wide_ref[r]
        east_shift = jnp.asarray(r, F32) - tile.east_centre
        return state[0:1] + east_shift, state[1:2] + north_of, state

    def feature_row(r, carry):
        east, north, state = place_of(r)
        size = state[4:5]
        reach = east * east + north * north
        near = jnp.concatenate([size, size * east, size * north, -(size * reach)], axis=0)
        near = jnp.concatenate(near_rows(pieces(near)), axis=0)
        extra = tile.depth - 24
        which = row_iota(extra, wide_lanes)
        is_row = which == r - 1
        is_col = which - tile.ring_rows == jnp.broadcast_to(block_of, (extra, wide_lanes)) - 1
        flags = jnp.where(is_row | is_col, jnp.broadcast_to(size, (extra, wide_lanes)), 0.0)
        near_ref[r] = jnp.concatenate([near, flags], axis=0).astype(BF16)
        return carry

    lax.fori_loop(0, tile.wide_rows, feature_row, 0, unroll=2)

    def own_features(east, north):
        reach = 1.0 - east * east - north * north
        own = jnp.concatenate([reach, 2.0 * east, 2.0 * north, jnp.ones_like(east)], axis=0)
        return jnp.concatenate(own_rows(pieces(own)), axis=0)

    def own_row(r, carry):
        east, north, state = place_of(r)
        own = own_features(east, north)
        own = jnp.concatenate([own, jnp.zeros((8, wide_lanes), F32)], axis=0)
        for c in range(tile.ring_cols):
            part = own[:, (c + 1) * LANES : (c + 2) * LANES]
            own_ref[r - 1, c] = part.T.astype(BF16)
        high, middle, _ = pieces(state[2:4, LANES : LANES + ring_lanes])
        ones = jnp.ones((1, ring_lanes), F32)
        blank = jnp.zeros((6, ring_lanes), F32)
        speeds = jnp.concatenate([high, ones, blank[:5], middle, blank], axis=0)
        drag_ref[r - 1] = speeds.astype(BF16)
        return carry

    lax.fori_loop(1, tile.ring_rows + 1, own_row, 0, unroll=2)

    def depth_block(r, c, keep):
        own = own_ref[r - 1, c - 1]
        lanes = pl.ds(pl.multiple_of((c - 1) * LANES, LANES), 3 * LANES)
        near = jnp.concatenate([near_ref[r + e - 1, 0:32, lanes] for e in range(3)], axis=1)
        all_close = jnp.maximum(jnp.dot(own, near, preferred_element_type=F32), 0.0)
        total = jnp.zeros((LANES, LANES), F32)
        thirds = []
        for block in range(9):
            close = all_close[:, block * LANES : (block + 1) * LANES]
            second = close * close
            third = second * close
            total = total + third
            if keep is not None:
                thirds.append(third.astype(BF16))
                high = second.astype(BF16)
                low = (second - high.astype(F32)).astype(BF16)
                pair_ref[keep, :, block * LANES : (block + 1) * LANES] = high
                pair_ref[keep, :, (9 + block) * LANES : (10 + block) * LANES] = low
        depth = lane_sums(total) * (1.0 / LANES)
        depth_ref[r - 1, 0:1, pl.ds(pl.multiple_of((c - 1) * LANES, LANES), LANES)] = depth
        if keep is not None:
            lanes = pl.ds(pl.multiple_of((c - 2) * LANES, LANES), 3 * LANES)
            speeds = jnp.concatenate([drag_ref[r + e - 2, :, lanes] for e in range(3)], axis=1)
            drag = across(speeds, jnp.concatenate(thirds, axis=1))
            lanes = pl.ds(pl.multiple_of((c - 2) * LANES, LANES), LANES)
            sums_ref[r - 2, 8:16, lanes] = drag[0:8] + drag[8:16]

    def own_depth(k, carry):
        depth_block(k // cols + 2, k % cols + 2, k)
        return carry

    lax.fori_loop(0, rows * cols, own_depth, 0, unroll=16)

    if with_bound:
        pair_copy = pltpu.make_async_copy(kept[1], pair_all, copies.at[2])
        pair_copy.start()

    def side_depth(k, carry):
        depth_block(1 + (rows + 1) * (k // tile.ring_cols), 1 + k % tile.ring_cols, None)
        return carry

    lax.fori_loop(0, 2 * tile.ring_cols, side_depth, 0, unroll=10)

    def end_depth(k, carry):
        depth_block(2 + k // 2, 1 + (cols + 1) * (k % 2), None)
        return carry

    lax.fori_loop(0, 2 * rows, end_depth, 0, unroll=8)

    def column_row(r, carry):
        east, north, state = place_of(r)
        inner = slice(LANES, LANES + ring_lanes)
        east, north, state = east[:, inner], north[:, inner], state[:, inner]
        size = state[4:5]
        heavy = size * depth_ref[r - 1, 0:1]
        blank = jnp.zeros((2, ring_lanes), F32)
        first = [size, heavy, size * east, size * north, heavy * east, heavy * north, blank]
        first = jnp.concatenate(first, axis=0)
        if with_bound:
            exact_ref[r - 1] = first
        heavy_ref[r - 1] = jnp.concatenate(pieces(first), axis=0).astype(BF16)
        return carry

    lax.fori_loop(1, tile.ring_rows + 1, column_row, 0, unroll=2)

    if with_bound:
        place_copy.wait()
        cell_copy.wait()
        groups = place_ref.shape[1] // GROUP
        cell = cell_ref[...]
        local = cell.astype(F32) - shift_ref[...]
        east = place_ref[0:1] + (local[0:1] + (2.0 - tile.east_centre))
        north = place_ref[1:2] + (local[1:2] + (2.0 - tile.north_centre))
        lanes = place_ref.shape[1]
        extra = tile.depth - 24
        which = row_iota(extra, lanes).astype(F32)
        apart_row = jnp.abs(which - (local[0:1] + 1.0))
        apart_col = jnp.abs(which - tile.ring_rows - (local[1:2] + 1.0))
        apart = jnp.where(which < tile.ring_rows - 0.5, apart_row, apart_col)
        apart = jnp.where(which < tile.mask_rows - 0.5, apart, 0.0)
        masks = jnp.where(apart > 1.5, -FAR, 0.0)
        bound = jnp.concatenate([own_features(east, north), masks], axis=0)
        for group in range(groups):
            back_ref[group] = bound[:, group * GROUP : (group + 1) * GROUP].T.astype(BF16)

        def bound_group(group, carry):
            own = back_ref[group]
            totals = [jnp.zeros((GROUP, LANES), F32) for _ in range(3)]
            for r in range(tile.ring_rows):
                near = near_ref[r + 1, :, LANES : LANES + ring_lanes]
                close = jnp.maximum(jnp.dot(own, near, preferred_element_type=F32), 0.0)
                for c in range(tile.ring_cols):
                    lanes = slice(c * LANES, (c + 1) * LANES)
                    second = close[:, lanes] * close[:, lanes]
                    for which, row in enumerate((1, 4, 5)):
                        weight = exact_ref[r, row : row + 1, lanes]
                        totals[which] = totals[which] + second * weight
            for which in range(3):
                total_ref[which, pl.ds(pl.multiple_of(group * GROUP, GROUP), GROUP)] = totals[which]
            return carry

        lax.fori_loop(0, groups, bound_group, 0)
        merged = []
        for which in range(3):
            parts = []
            for group in range(lanes // LANES):
                parts.append(lane_sums(total_ref[which, group * LANES : (group + 1) * LANES]))
            merged.append(jnp.concatenate(parts, axis=1))
        factor = 6.0 * gravity / LANES
        force_east = factor * (east * merged[0] - merged[1])
        force_north = factor * (north * merged[0] - merged[2])
        cell_place = cell.astype(F32)
        torque = (cell_place[0:1] + place_ref[0:1]) * force_north
        torque = torque - (cell_place[1:2] + place_ref[1:2]) * force_east
        chosen = row_iota(8, lanes) == slot_ref[...]
        columns = []
        for values in (force_east, force_north, torque):
            picked = jnp.where(chosen, jnp.broadcast_to(values, (8, lanes)), 0.0)
            columns.append(jnp.sum(picked, axis=1, keepdims=True))
        lane = lax.broadcasted_iota(jnp.int32, (8, LANES), 1)
        result = jnp.where(lane == 0, columns[0], jnp.where(lane == 1, columns[1], columns[2]))
        sums_out[...] = result
        pair_copy.wait()


def push_half(tile, wide_ref, kept, state_out, final_out=None, row_copy=None):
    depth_ref, pair_ref, heavy_ref, sums_ref = kept
    rows, cols = tile.rows, tile.cols
    north_of = lane_block(tile.wide_cols * LANES).astype(F32) - tile.north_centre

    def place_of(r):
        state = wide_ref[r]
        east_shift = jnp.asarray(r, F32) - tile.east_centre
        return state[0:1] + east_shift, state[1:2] + north_of, state

    def push_block(r, c):
        lanes = slice(c * LANES, (c + 3) * LANES)
        near = [heavy_ref[r + e, :, lanes] for e in range(3)]
        total = across(jnp.concatenate(near + near, axis=1), pair_ref[r * cols + c])
        merged = total[0:8] + total[8:16] + total[16:24]
        sums_ref[r, 0:8, c * LANES : (c + 1) * LANES] = merged

    def push_row(r, carry):
        if final_out is not None:
            row_copy(r).wait()
        for c in range(cols):
            push_block(r, c)
        return carry

    lax.fori_loop(0, rows, push_row, 0)

    def update_row(r, carry):
        east, north, state = place_of(r + 2)
        inner = slice(2 * LANES, (2 + cols) * LANES)
        east, north, state = east[:, inner], north[:, inner], state[:, inner]
        sums = sums_ref[r]
        depth = depth_ref[r + 1, 0:1, LANES : (1 + cols) * LANES]
        speed_east, speed_north = state[2:3], state[3:4]
        heavy = depth * sums[0:1] + sums[1:2]
        push_east = heavy * east - depth * sums[2:3] - sums[4:5]
        push_north = heavy * north - depth * sums[3:4] - sums[5:6]
        drag_east = sums[8:9] - speed_east * sums[10:11]
        drag_north = sums[9:10] - speed_north * sums[10:11]
        scale = 3.0 * gravity / LANES
        thin = viscosity / LANES
        speed_east = speed_east + step_time * (scale * push_east + thin * drag_east)
        speed_north = speed_north + step_time * (scale * push_north + thin * drag_north)
        east = state[0:1] + step_time * speed_east
        north = state[1:2] + step_time * speed_north
        if state_out is not None:
            blank = jnp.zeros((STATE_ROWS - 5, cols * LANES), F32)
            new = [east, north, speed_east, speed_north, state[4:5], blank]
            state_out[r] = jnp.concatenate(new, axis=0)
        else:
            position_out, velocity_out, depth_out = final_out
            for c in range(cols):
                lanes = slice(c * LANES, (c + 1) * LANES)
                position_out[r, 0, c : c + 1] = east[:, lanes]
                position_out[r, 1, c : c + 1] = north[:, lanes]
                velocity_out[r, 0, c : c + 1] = speed_east[:, lanes]
                velocity_out[r, 1, c : c + 1] = speed_north[:, lanes]
                depth_out[r, c : c + 1] = depth[:, lanes]
        return carry

    lax.fori_loop(0, rows, update_row, 0, unroll=2)


def kept_shapes(tile):
    rows, cols = tile.rows, tile.cols
    return [
        ((tile.ring_rows, 8, tile.ring_cols * LANES), F32),
        ((rows * cols, LANES, 18 * LANES), BF16),
        ((tile.ring_rows, 24, tile.ring_cols * LANES), BF16),
        ((rows, 16, cols * LANES), F32),
    ]


def scratch_shapes(tile):
    return [
        ((tile.wide_rows, tile.depth, tile.wide_cols * LANES), BF16),
        ((tile.ring_rows, tile.ring_cols, LANES, 32), BF16),
        ((tile.ring_rows, 16, tile.ring_cols * LANES), BF16),
    ]


def in_vmem(shapes):
    return [pltpu.VMEM(shape, dtype) for shape, dtype in shapes]


VMEM_SPEC = pl.BlockSpec(memory_space=pltpu.VMEM)
LIMIT = 52 << 20


def run_substep(tile, wide):
    def body(wide_ref, state_out, *refs):
        kept, scratch = refs[:4], refs[4:]
        depth_half(tile, wide_ref, None, kept, scratch)
        push_half(tile, wide_ref, kept, state_out)

    return pl.pallas_call(
        body,
        out_shape=jax.ShapeDtypeStruct((tile.rows, STATE_ROWS, tile.cols * LANES), F32),
        in_specs=[VMEM_SPEC],
        out_specs=VMEM_SPEC,
        scratch_shapes=in_vmem(kept_shapes(tile) + scratch_shapes(tile)),
        compiler_params=pltpu.CompilerParams(vmem_limit_bytes=LIMIT),
        name="substep",
    )(wide)


HBM_SPEC = pl.BlockSpec(memory_space=pltpu.HBM)


def in_hbm(array):
    return pltpu.with_memory_space_constraint(array, pltpu.HBM)


def run_bound(tile, wide, bound):
    place, cell, slot, shift = bound
    lanes = place.shape[1]
    back = [
        ((lanes // GROUP, GROUP, tile.depth), BF16),
        ((3, lanes, LANES), F32),
        ((tile.ring_rows, 8, tile.ring_cols * LANES), F32),
        (place.shape, F32),
        (cell.shape, jnp.int32),
    ]
    depth_shape, pair_shape, heavy_shape, sums_shape = kept_shapes(tile)

    def body(wide_ref, place_all, cell_all, slot_ref, shift_ref, sums_out, *refs):
        depth_ref, pair_all, heavy_ref, sums_ref, pair_ref = refs[:5]
        scratch, back_refs, copies = refs[5:8], refs[8:13], refs[13]
        bound_refs = back_refs[3:] + (slot_ref, shift_ref, sums_out) + back_refs[:3]
        bound_refs = bound_refs + (place_all, cell_all, pair_all, copies)
        depth_half(tile, wide_ref, bound_refs, (depth_ref, pair_ref, heavy_ref, sums_ref), scratch)

    outs = [((8, LANES), F32), depth_shape, pair_shape, heavy_shape, sums_shape]
    return pl.pallas_call(
        body,
        out_shape=[jax.ShapeDtypeStruct(shape, dtype) for shape, dtype in outs],
        in_specs=[VMEM_SPEC, HBM_SPEC, HBM_SPEC, VMEM_SPEC, VMEM_SPEC],
        out_specs=[VMEM_SPEC, VMEM_SPEC, HBM_SPEC, VMEM_SPEC, VMEM_SPEC],
        scratch_shapes=in_vmem([pair_shape] + scratch_shapes(tile) + back) + [pltpu.SemaphoreType.DMA((3,))],
        compiler_params=pltpu.CompilerParams(vmem_limit_bytes=LIMIT),
        name="depth_bound",
    )(wide, in_hbm(place), in_hbm(cell), slot, shift)


def run_push(tile, wide, kept):
    rows, cols = tile.rows, tile.cols
    pair = jax.ShapeDtypeStruct((rows, 2, cols, LANES), F32)
    kept_in = kept_shapes(tile)

    def body(wide_ref, depth_ref, pair_all, heavy_ref, drag_sums, position, velocity, depth, *refs):
        pair_ref, sums_ref, copies = refs

        def row_copy(r):
            part = pl.ds(r * cols, cols)
            return pltpu.make_async_copy(pair_all.at[part], pair_ref.at[part], copies.at[r])

        for r in range(rows):
            row_copy(r).start()
        sums_ref[...] = drag_sums[...]
        kept_refs = (depth_ref, pair_ref, heavy_ref, sums_ref)
        push_half(tile, wide_ref, kept_refs, None, (position, velocity, depth), row_copy)

    return pl.pallas_call(
        body,
        out_shape=[pair, pair, jax.ShapeDtypeStruct((rows, cols, LANES), F32)],
        in_specs=[VMEM_SPEC, VMEM_SPEC, HBM_SPEC, VMEM_SPEC, VMEM_SPEC],
        out_specs=[VMEM_SPEC] * 3,
        scratch_shapes=in_vmem([kept_in[1], kept_in[3]]) + [pltpu.SemaphoreType.DMA((rows,))],
        compiler_params=pltpu.CompilerParams(vmem_limit_bytes=32 << 20),
        cost_estimate=pl.CostEstimate(flops=8 * 10**9, bytes_accessed=2 * 10**7, transcendentals=0),
        name="push",
    )(wide, kept[0], in_hbm(kept[1]), *kept[2:])


def swapped_edges(low_edge, high_edge, axis):
    count = lax.axis_size(axis)
    odd = lax.axis_index(axis) % 2 == 1
    first = [(i, i ^ 1) for i in range(count)]
    second = [(i, ((i + 1) ^ 1) - 1) for i in range(1, count - 1)]
    to_first = jnp.where(odd, low_edge, high_edge)
    to_second = jnp.where(odd, high_edge, low_edge)
    from_second = lax.ppermute(to_second, axis, second)
    from_first = lax.ppermute(to_first, axis, first)
    low = jnp.where(odd, from_first, from_second)
    high = jnp.where(odd, from_second, from_first)
    return low, high


def with_halo(state):
    side = 2 * LANES
    low, high = swapped_edges(state[:, :, :side], state[:, :, -side:], ALONG_Y)
    state = jnp.concatenate([low, state, high], axis=2)
    low, high = swapped_edges(state[:2], state[-2:], "gx")
    return jnp.concatenate([low, state, high], axis=0)


def initial_state(position, velocity, volume):
    rows, _, cols, lanes = position.shape

    def body(position_ref, velocity_ref, volume_ref, state_out):
        blank = jnp.zeros((STATE_ROWS - 5, LANES), F32)
        for r in range(rows):
            volumes = volume_ref[r]
            size = jnp.exp(jnp.log(volumes) * (1.0 / 3.0))
            square = size * size
            size = size - (square * size - volumes) / (3.0 * square)
            for c in range(cols):
                row = slice(c, c + 1)
                new = [
                    position_ref[r, 0, row],
                    position_ref[r, 1, row],
                    velocity_ref[r, 0, row],
                    velocity_ref[r, 1, row],
                    size[row],
                    blank,
                ]
                state_out[r, :, c * LANES : (c + 1) * LANES] = jnp.concatenate(new, axis=0)

    return pl.pallas_call(
        body,
        out_shape=pltpu.VMEM((rows, STATE_ROWS, cols * lanes), F32),
        in_specs=[VMEM_SPEC] * 3,
        out_specs=VMEM_SPEC,
        name="initial",
    )(position, velocity, volume)


def on_device(
    fluid_position,
    fluid_velocity,
    fluid_volume,
    bound_offset,
    bound_cell,
    bound_body,
    body_state,
    mass_inverse,
    inertia_inverse,
):
    rows, cols = fluid_position.shape[0], fluid_position.shape[2]
    tile = Tile(rows, cols)
    shard_bodies = body_state.shape[1]
    owners = lax.axis_size("body")
    devices = lax.axis_size(EVERY)
    tiles_north = lax.axis_size(ALONG_Y)
    body_total = shard_bodies * owners
    own_bodies = body_total // devices
    sharing = devices // owners
    me = lax.axis_index(EVERY)

    state = initial_state(fluid_position, fluid_velocity, fluid_volume)
    shift = jnp.stack([lax.axis_index("gx") * rows, lax.axis_index(ALONG_Y) * cols])
    shift = shift.astype(F32)[:, None]
    slot = bound_body - me * own_bodies
    slot = jnp.where(slot < 0, slot + 2 * own_bodies, slot)

    bodies = jnp.concatenate([body_state, mass_inverse[None], inertia_inverse[None]], axis=0)
    by_home = bodies.reshape(7, sharing, own_bodies)
    place = lax.broadcasted_iota(jnp.int32, (1, sharing, 1), 1) % tiles_north
    after = jnp.concatenate([by_home[:, 1:], by_home[:, -1:]], axis=1)
    before = jnp.concatenate([by_home[:, :1], by_home[:, :-1]], axis=1)
    beside = jnp.where(place == tiles_north - 1, before, after)
    params = jnp.concatenate([by_home, beside], axis=2)
    params = jnp.transpose(params, (1, 0, 2)).reshape(sharing, 7 * 2 * own_bodies)
    params = jnp.concatenate([params] * owners, axis=0)

    for _ in range(SUBSTEPS - 1):
        state = run_substep(tile, with_halo(state))
    bound = (bound_offset, bound_cell, slot[None], shift)
    wide = with_halo(state)
    sums, *kept = run_bound(tile, wide, bound)

    partial = sums[:, :3].T.reshape(1, 6 * own_bodies)
    message = jnp.concatenate([jnp.broadcast_to(partial, (devices, 6 * own_bodies)), params], axis=1)
    received = lax.all_to_all(message, EVERY, 0, 0, tiled=True)
    position, velocity, depth = run_push(tile, wide, kept)
    partials = received[:, : 6 * own_bodies].reshape(devices, 3, 2 * own_bodies)
    partials = jnp.transpose(partials, (1, 0, 2))
    own_part, beside_part = partials[:, :, :own_bodies], partials[:, :, own_bodies:]
    place = lax.broadcasted_iota(jnp.int32, (1, devices, 1), 1) % tiles_north
    from_before = jnp.concatenate([beside_part[:, :1], beside_part[:, :-1]], axis=1)
    from_after = jnp.concatenate([beside_part[:, 1:], beside_part[:, -1:]], axis=1)
    totals = own_part + jnp.where(place > 0, from_before, 0.0)
    totals = totals + jnp.where(place == tiles_north - 2, from_after, 0.0)

    def integrate(state_of, mass_of, inertia_of, sums_of):
        span = step_time * SUBSTEPS
        east = state_of[2] + span * mass_of * sums_of[0]
        north = state_of[3] + span * mass_of * sums_of[1]
        torque = sums_of[2] - (state_of[0] * sums_of[1] - state_of[1] * sums_of[0])
        return jnp.stack([east, north, state_of[4] + span * inertia_of * torque])

    shard = lax.axis_index("body")
    shard_sums = lax.dynamic_slice_in_dim(totals, shard * sharing, sharing, axis=1)
    shard_sums = shard_sums.reshape(3, shard_bodies)
    motion = integrate(body_state, mass_inverse, inertia_inverse, shard_sums)

    tile_place = lax.axis_index(ALONG_Y)
    other = jnp.where(tile_place == tiles_north - 1, me - 1, me + 1)
    mine = lax.dynamic_slice_in_dim(totals, me, 1, axis=1)[:, 0]
    theirs = lax.dynamic_slice_in_dim(totals, other, 1, axis=1)[:, 0]
    local_sums = jnp.concatenate([mine, theirs], axis=1)
    local = lax.dynamic_slice_in_dim(received, me // sharing, 1, axis=0)[0, 6 * own_bodies :]
    local = local.reshape(7, 2 * own_bodies)
    local_motion = integrate(local[:5], local[5], local[6], local_sums)
    table = jnp.concatenate([local_motion, local[:2]], axis=0)
    chosen = slot[None, :, None] == jnp.arange(2 * own_bodies, dtype=jnp.int32)
    picked = jnp.sum(jnp.where(chosen, table[:, None, :], 0.0), axis=-1)
    place_east = bound_cell[0].astype(F32) + bound_offset[0]
    place_north = bound_cell[1].astype(F32) + bound_offset[1]
    bound_velocity = jnp.stack(
        [
            picked[0] - picked[2] * (place_north - picked[4]),
            picked[1] + picked[2] * (place_east - picked[3]),
        ]
    )
    return position, velocity, depth, motion, bound_velocity


def solution(mesh):
    return jax.shard_map(
        on_device,
        mesh=mesh,
        in_specs=(
            P("gx", None, ("gy", "body"), None),
            P("gx", None, ("gy", "body"), None),
            P("gx", ("gy", "body"), None),
            P(None, ("gx", "gy", "body")),
            P(None, ("gx", "gy", "body")),
            P(("gx", "gy", "body")),
            P(None, "body"),
            P("body"),
            P("body"),
        ),
        out_specs=(
            P("gx", None, ("gy", "body"), None),
            P("gx", None, ("gy", "body"), None),
            P("gx", ("gy", "body"), None),
            P(None, "body"),
            P(None, ("gx", "gy", "body")),
        ),
        check_vma=False,
    )
```

```python
import jax
import jax.numpy as jnp
from jax import lax
from jax.experimental import pallas as pl
from jax.experimental.pallas import tpu as pltpu
from jax.sharding import PartitionSpec as P

SUBSTEPS = 3

gravity = 3.0
viscosity = 1.0
step_time = 0.05

ALONG_Y = ("gy", "body")
EVERY = ("gx", "gy", "body")
LANES = 128
GROUP = 128
FAR = 4096.0
F32 = jnp.float32
BF16 = jnp.bfloat16

STATE_ROWS = 8


def pieces(values):
    high = values.astype(BF16).astype(F32)
    rest = values - high
    middle = rest.astype(BF16).astype(F32)
    low = (rest - middle).astype(BF16).astype(F32)
    return high, middle, low


def near_rows(parts):
    high, middle, low = parts
    return [high, middle, low, high, middle, high]


def own_rows(parts):
    high, middle, low = parts
    return [high, high, high, middle, middle, low]


def row_iota(rows, lanes):
    return lax.broadcasted_iota(jnp.int32, (rows, lanes), 0)


def across(rows, pairs):
    dims = (((1,), (1,)), ((), ()))
    return lax.dot_general(rows, pairs, dims, preferred_element_type=F32)


def lane_sums(values):
    return jnp.sum(values.T, axis=0, keepdims=True)


class Tile:
    def __init__(self, rows, cols):
        self.rows, self.cols = rows, cols
        self.wide_rows, self.wide_cols = rows + 4, cols + 4
        self.ring_rows, self.ring_cols = rows + 2, cols + 2
        self.mask_rows = self.ring_rows + self.ring_cols
        self.depth = -(-(24 + self.mask_rows) // 16) * 16
        self.east_centre = float(self.wide_rows // 2)
        self.north_centre = float(self.wide_cols // 2)


def lane_block(ref_lanes):
    return lax.broadcasted_iota(jnp.int32, (1, ref_lanes), 1) // LANES


def depth_half(tile, wide_ref, bound_refs, kept, scratch):
    with_bound = bound_refs is not None
    if with_bound:
        (place_ref, cell_ref, slot_ref, shift_ref, sums_out, back_ref, total_ref, exact_ref) = bound_refs[:8]
        place_all, cell_all, pair_all, side_all, copies = bound_refs[8:]
        place_copy = pltpu.make_async_copy(place_all, place_ref, copies.at[0])
        cell_copy = pltpu.make_async_copy(cell_all, cell_ref, copies.at[1])
        place_copy.start()
        cell_copy.start()
    depth_ref, pair_ref, side_ref, heavy_ref, sums_ref = kept
    near_ref, own_ref, drag_ref = scratch
    rows, cols = tile.rows, tile.cols
    wide_lanes = tile.wide_cols * LANES
    ring_lanes = tile.ring_cols * LANES

    block_of = lane_block(wide_lanes)
    north_of = block_of.astype(F32) - tile.north_centre

    def place_of(r):
        state = wide_ref[r]
        east_shift = jnp.asarray(r, F32) - tile.east_centre
        return state[0:1] + east_shift, state[1:2] + north_of, state

    def feature_row(r, carry):
        east, north, state = place_of(r)
        size = state[4:5]
        reach = east * east + north * north
        near = jnp.concatenate([size, size * east, size * north, -(size * reach)], axis=0)
        near = jnp.concatenate(near_rows(pieces(near)), axis=0)
        extra = tile.depth - 24
        which = row_iota(extra, wide_lanes)
        is_row = which == r - 1
        is_col = which - tile.ring_rows == jnp.broadcast_to(block_of, (extra, wide_lanes)) - 1
        flags = jnp.where(is_row | is_col, jnp.broadcast_to(size, (extra, wide_lanes)), 0.0)
        near_ref[r] = jnp.concatenate([near, flags], axis=0).astype(BF16)
        return carry

    lax.fori_loop(0, tile.wide_rows, feature_row, 0, unroll=2)

    def own_features(east, north):
        reach = 1.0 - east * east - north * north
        own = jnp.concatenate([reach, 2.0 * east, 2.0 * north, jnp.ones_like(east)], axis=0)
        return jnp.concatenate(own_rows(pieces(own)), axis=0)

    def own_row(r, carry):
        east, north, state = place_of(r)
        own = own_features(east, north)
        own = jnp.concatenate([own, jnp.zeros((8, wide_lanes), F32)], axis=0)
        for c in range(tile.ring_cols):
            part = own[:, (c + 1) * LANES : (c + 2) * LANES]
            own_ref[r - 1, c] = part.T.astype(BF16)
        high, middle, _ = pieces(state[2:4, LANES : LANES + ring_lanes])
        ones = jnp.ones((1, ring_lanes), F32)
        blank = jnp.zeros((6, ring_lanes), F32)
        speeds = jnp.concatenate([high, ones, blank[:5], middle, blank], axis=0)
        drag_ref[r - 1] = speeds.astype(BF16)
        return carry

    lax.fori_loop(1, tile.ring_rows + 1, own_row, 0, unroll=2)

    def store_pieces(ref, index, place, places, values):
        high = values.astype(BF16)
        low = (values - high.astype(F32)).astype(BF16)
        ref[index, :, place * LANES : (place + 1) * LANES] = high
        ref[index, :, (places + place) * LANES : (places + place + 1) * LANES] = low

    def depth_block(r, c, keep, side=None):
        own = own_ref[r - 1, c - 1]
        lanes = pl.ds(pl.multiple_of((c - 1) * LANES, LANES), 3 * LANES)
        near = jnp.concatenate([near_ref[r + e - 1, 0:32, lanes] for e in range(3)], axis=1)
        all_close = jnp.maximum(jnp.dot(own, near, preferred_element_type=F32), 0.0)
        total = jnp.zeros((LANES, LANES), F32)
        thirds = []
        for block in range(9):
            close = all_close[:, block * LANES : (block + 1) * LANES]
            second = close * close
            third = second * close
            total = total + third
            if keep is not None:
                thirds.append(third.astype(BF16))
                store_pieces(pair_ref, keep, block, 9, second)
            elif block in side[1]:
                store_pieces(side_ref, side[0], side[1].index(block), 3, second)
        depth = lane_sums(total) * (1.0 / LANES)
        depth_ref[r - 1, 0:1, pl.ds(pl.multiple_of((c - 1) * LANES, LANES), LANES)] = depth
        if keep is not None:
            lanes = pl.ds(pl.multiple_of((c - 2) * LANES, LANES), 3 * LANES)
            speeds = jnp.concatenate([drag_ref[r + e - 2, :, lanes] for e in range(3)], axis=1)
            drag = across(speeds, jnp.concatenate(thirds, axis=1))
            lanes = pl.ds(pl.multiple_of((c - 2) * LANES, LANES), LANES)
            sums_ref[r - 2, 8:16, lanes] = drag[0:8] + drag[8:16]

    def own_depth(k, carry):
        depth_block(k // cols + 2, k % cols + 2, k)
        return carry

    lax.fori_loop(0, rows * cols, own_depth, 0, unroll=16)

    if with_bound:
        pair_copy = pltpu.make_async_copy(pair_ref, pair_all, copies.at[2])
        pair_copy.start()

    def side_depth(c, carry):
        depth_block(1, 1 + c, None, (c, (6, 7, 8)))
        depth_block(rows + 2, 1 + c, None, (tile.ring_cols + c, (0, 1, 2)))
        return carry

    lax.fori_loop(0, tile.ring_cols, side_depth, 0, unroll=5)

    def end_depth(k, carry):
        depth_block(2 + k, 1, None, (2 * tile.ring_cols + k, (2, 5, 8)))
        depth_block(2 + k, cols + 2, None, (2 * tile.ring_cols + rows + k, (0, 3, 6)))
        return carry

    lax.fori_loop(0, rows, end_depth, 0, unroll=4)

    if with_bound:
        side_copy = pltpu.make_async_copy(side_ref, side_all, copies.at[3])
        side_copy.start()

    def column_row(r, carry):
        east, north, state = place_of(r)
        inner = slice(LANES, LANES + ring_lanes)
        east, north, state = east[:, inner], north[:, inner], state[:, inner]
        size = state[4:5]
        deep = size * depth_ref[r - 1, 0:1]
        blank = jnp.zeros((2, ring_lanes), F32)
        first = [size, deep, size * east, size * north, deep * east, deep * north, blank]
        first = jnp.concatenate(first, axis=0)
        if with_bound:
            exact_ref[r - 1] = first
        heavy = pieces(first * (size * size))
        heavy_ref[r - 1] = jnp.concatenate(heavy, axis=0).astype(BF16)
        return carry

    lax.fori_loop(1, tile.ring_rows + 1, column_row, 0, unroll=2)

    if with_bound:
        place_copy.wait()
        cell_copy.wait()
        groups = place_ref.shape[1] // GROUP
        cell = cell_ref[...]
        local = cell.astype(F32) - shift_ref[...]
        east = place_ref[0:1] + (local[0:1] + (2.0 - tile.east_centre))
        north = place_ref[1:2] + (local[1:2] + (2.0 - tile.north_centre))
        lanes = place_ref.shape[1]
        extra = tile.depth - 24
        which = row_iota(extra, lanes).astype(F32)
        apart_row = jnp.abs(which - (local[0:1] + 1.0))
        apart_col = jnp.abs(which - tile.ring_rows - (local[1:2] + 1.0))
        apart = jnp.where(which < tile.ring_rows - 0.5, apart_row, apart_col)
        apart = jnp.where(which < tile.mask_rows - 0.5, apart, 0.0)
        masks = jnp.where(apart > 1.5, -FAR, 0.0)
        bound = jnp.concatenate([own_features(east, north), masks], axis=0)
        for group in range(groups):
            back_ref[group] = bound[:, group * GROUP : (group + 1) * GROUP].T.astype(BF16)

        def bound_group(group, carry):
            own = back_ref[group]
            totals = [jnp.zeros((GROUP, LANES), F32) for _ in range(3)]
            for r in range(tile.ring_rows):
                near = near_ref[r + 1, :, LANES : LANES + ring_lanes]
                close = jnp.maximum(jnp.dot(own, near, preferred_element_type=F32), 0.0)
                for c in range(tile.ring_cols):
                    lanes = slice(c * LANES, (c + 1) * LANES)
                    second = close[:, lanes] * close[:, lanes]
                    for which, row in enumerate((1, 4, 5)):
                        weight = exact_ref[r, row : row + 1, lanes]
                        totals[which] = totals[which] + second * weight
            for which in range(3):
                total_ref[which, pl.ds(pl.multiple_of(group * GROUP, GROUP), GROUP)] = totals[which]
            return carry

        lax.fori_loop(0, groups, bound_group, 0)
        merged = []
        for which in range(3):
            parts = []
            for group in range(lanes // LANES):
                parts.append(lane_sums(total_ref[which, group * LANES : (group + 1) * LANES]))
            merged.append(jnp.concatenate(parts, axis=1))
        factor = 6.0 * gravity / LANES
        force_east = factor * (east * merged[0] - merged[1])
        force_north = factor * (north * merged[0] - merged[2])
        cell_place = cell.astype(F32)
        torque = (cell_place[0:1] + place_ref[0:1]) * force_north
        torque = torque - (cell_place[1:2] + place_ref[1:2]) * force_east
        chosen = row_iota(8, lanes) == slot_ref[...]
        columns = []
        for values in (force_east, force_north, torque):
            picked = jnp.where(chosen, jnp.broadcast_to(values, (8, lanes)), 0.0)
            columns.append(jnp.sum(picked, axis=1, keepdims=True))
        lane = lax.broadcasted_iota(jnp.int32, (8, LANES), 1)
        result = jnp.where(lane == 0, columns[0], jnp.where(lane == 1, columns[1], columns[2]))
        sums_out[...] = result
        pair_copy.wait()
        side_copy.wait()


def push_half(tile, wide_ref, kept, state_out, final_out=None, row_copy=None):
    depth_ref, pair_ref, side_ref, heavy_ref, sums_ref = kept
    rows, cols = tile.rows, tile.cols
    north_of = lane_block(tile.wide_cols * LANES).astype(F32) - tile.north_centre

    def place_of(r):
        state = wide_ref[r]
        east_shift = jnp.asarray(r, F32) - tile.east_centre
        return state[0:1] + east_shift, state[1:2] + north_of, state

    def weights_from(r, c, e, f):
        from_row, from_col = r + e, c + f
        if 1 <= from_row <= rows and 1 <= from_col <= cols:
            ref, index = pair_ref, (from_row - 1) * cols + from_col - 1
            place, places = (2 - e) * 3 + 2 - f, 9
        elif from_row in (0, rows + 1):
            ref, index = side_ref, from_col + (tile.ring_cols if from_row else 0)
            place, places = 2 - f, 3
        else:
            ref, index = side_ref, 2 * tile.ring_cols + from_row - 1 + (rows if from_col else 0)
            place, places = 2 - e, 3
        high = ref[index, :, place * LANES : (place + 1) * LANES]
        low = ref[index, :, (places + place) * LANES : (places + place + 1) * LANES]
        return high, low

    def push_block(r, c):
        lanes = slice(c * LANES, (c + 3) * LANES)
        near = [heavy_ref[r + e, :, lanes] for e in range(3)]
        highs, lows = zip(*[weights_from(r, c, e, f) for e in range(3) for f in range(3)])
        weights = jnp.concatenate(highs + lows, axis=0)
        total = jnp.dot(jnp.concatenate(near + near, axis=1), weights, preferred_element_type=F32)
        merged = total[0:8] + total[8:16] + total[16:24]
        sums_ref[r, 0:8, c * LANES : (c + 1) * LANES] = merged

    for r in range(rows):
        if final_out is not None:
            for step in {0: range(min(2, rows) + 1), rows - 1: ()}.get(r, (r + 2,)):
                row_copy(step).wait()
        for c in range(cols):
            push_block(r, c)

    def update_row(r, carry):
        east, north, state = place_of(r + 2)
        inner = slice(2 * LANES, (2 + cols) * LANES)
        east, north, state = east[:, inner], north[:, inner], state[:, inner]
        drag = sums_ref[r, 8:16]
        sums = sums_ref[r, 0:8] / (state[4:5] * state[4:5])
        depth = depth_ref[r + 1, 0:1, LANES : (1 + cols) * LANES]
        speed_east, speed_north = state[2:3], state[3:4]
        heavy = depth * sums[0:1] + sums[1:2]
        push_east = heavy * east - depth * sums[2:3] - sums[4:5]
        push_north = heavy * north - depth * sums[3:4] - sums[5:6]
        drag_east = drag[0:1] - speed_east * drag[2:3]
        drag_north = drag[1:2] - speed_north * drag[2:3]
        scale = 3.0 * gravity / LANES
        thin = viscosity / LANES
        speed_east = speed_east + step_time * (scale * push_east + thin * drag_east)
        speed_north = speed_north + step_time * (scale * push_north + thin * drag_north)
        east = state[0:1] + step_time * speed_east
        north = state[1:2] + step_time * speed_north
        if state_out is not None:
            blank = jnp.zeros((STATE_ROWS - 5, cols * LANES), F32)
            new = [east, north, speed_east, speed_north, state[4:5], blank]
            state_out[r] = jnp.concatenate(new, axis=0)
        else:
            position_out, velocity_out, depth_out = final_out
            for c in range(cols):
                lanes = slice(c * LANES, (c + 1) * LANES)
                position_out[r, 0, c : c + 1] = east[:, lanes]
                position_out[r, 1, c : c + 1] = north[:, lanes]
                velocity_out[r, 0, c : c + 1] = speed_east[:, lanes]
                velocity_out[r, 1, c : c + 1] = speed_north[:, lanes]
                depth_out[r, c : c + 1] = depth[:, lanes]
        return carry

    lax.fori_loop(0, rows, update_row, 0, unroll=2)


def kept_shapes(tile):
    rows, cols = tile.rows, tile.cols
    return [
        ((tile.ring_rows, 8, tile.ring_cols * LANES), F32),
        ((rows * cols, LANES, 18 * LANES), BF16),
        ((2 * (tile.ring_cols + rows), LANES, 6 * LANES), BF16),
        ((tile.ring_rows, 24, tile.ring_cols * LANES), BF16),
        ((rows, 16, cols * LANES), F32),
    ]


def scratch_shapes(tile):
    return [
        ((tile.wide_rows, tile.depth, tile.wide_cols * LANES), BF16),
        ((tile.ring_rows, tile.ring_cols, LANES, 32), BF16),
        ((tile.ring_rows, 16, tile.ring_cols * LANES), BF16),
    ]


def in_vmem(shapes):
    return [pltpu.VMEM(shape, dtype) for shape, dtype in shapes]


VMEM_SPEC = pl.BlockSpec(memory_space=pltpu.VMEM)
LIMIT = 52 << 20


def run_substep(tile, wide):
    def body(wide_ref, state_out, *refs):
        kept, scratch = refs[:5], refs[5:]
        depth_half(tile, wide_ref, None, kept, scratch)
        push_half(tile, wide_ref, kept, state_out)

    return pl.pallas_call(
        body,
        out_shape=jax.ShapeDtypeStruct((tile.rows, STATE_ROWS, tile.cols * LANES), F32),
        in_specs=[VMEM_SPEC],
        out_specs=VMEM_SPEC,
        scratch_shapes=in_vmem(kept_shapes(tile) + scratch_shapes(tile)),
        compiler_params=pltpu.CompilerParams(vmem_limit_bytes=LIMIT),
        name="substep",
    )(wide)


HBM_SPEC = pl.BlockSpec(memory_space=pltpu.HBM)


def in_hbm(array):
    return pltpu.with_memory_space_constraint(array, pltpu.HBM)


def run_bound(tile, wide, bound):
    place, cell, slot, shift = bound
    lanes = place.shape[1]
    back = [
        ((lanes // GROUP, GROUP, tile.depth), BF16),
        ((3, lanes, LANES), F32),
        ((tile.ring_rows, 8, tile.ring_cols * LANES), F32),
        (place.shape, F32),
        (cell.shape, jnp.int32),
    ]
    depth_shape, pair_shape, side_shape, heavy_shape, sums_shape = kept_shapes(tile)

    def body(wide_ref, place_all, cell_all, slot_ref, shift_ref, sums_out, *refs):
        depth_ref, pair_all, side_all, heavy_ref, sums_ref, pair_ref, side_ref = refs[:7]
        scratch, back_refs, copies = refs[7:10], refs[10:15], refs[15]
        bound_refs = back_refs[3:] + (slot_ref, shift_ref, sums_out) + back_refs[:3]
        bound_refs = bound_refs + (place_all, cell_all, pair_all, side_all, copies)
        kept_refs = (depth_ref, pair_ref, side_ref, heavy_ref, sums_ref)
        depth_half(tile, wide_ref, bound_refs, kept_refs, scratch)

    outs = [((8, LANES), F32), depth_shape, pair_shape, side_shape, heavy_shape, sums_shape]
    return pl.pallas_call(
        body,
        out_shape=[jax.ShapeDtypeStruct(shape, dtype) for shape, dtype in outs],
        in_specs=[VMEM_SPEC, HBM_SPEC, HBM_SPEC, VMEM_SPEC, VMEM_SPEC],
        out_specs=[VMEM_SPEC, VMEM_SPEC, HBM_SPEC, HBM_SPEC, VMEM_SPEC, VMEM_SPEC],
        scratch_shapes=in_vmem([pair_shape, side_shape] + scratch_shapes(tile) + back)
        + [pltpu.SemaphoreType.DMA((4,))],
        compiler_params=pltpu.CompilerParams(vmem_limit_bytes=LIMIT),
        name="depth_bound",
    )(wide, in_hbm(place), in_hbm(cell), slot, shift)


def run_push(tile, wide, kept):
    rows, cols = tile.rows, tile.cols
    pair = jax.ShapeDtypeStruct((rows, 2, cols, LANES), F32)
    kept_in = kept_shapes(tile)

    def body(wide_ref, depth_ref, pair_all, side_all, heavy_ref, drag_sums, *refs):
        position, velocity, depth, pair_ref, side_ref, sums_ref, copies = refs

        def row_copy(step):
            if step == 0:
                return pltpu.make_async_copy(side_all, side_ref, copies.at[0])
            part = pl.ds((step - 1) * cols, cols)
            return pltpu.make_async_copy(pair_all.at[part], pair_ref.at[part], copies.at[step])

        for step in range(rows + 1):
            row_copy(step).start()
        sums_ref[...] = drag_sums[...]
        kept_refs = (depth_ref, pair_ref, side_ref, heavy_ref, sums_ref)
        push_half(tile, wide_ref, kept_refs, None, (position, velocity, depth), row_copy)

    return pl.pallas_call(
        body,
        out_shape=[pair, pair, jax.ShapeDtypeStruct((rows, cols, LANES), F32)],
        in_specs=[VMEM_SPEC, VMEM_SPEC, HBM_SPEC, HBM_SPEC, VMEM_SPEC, VMEM_SPEC],
        out_specs=[VMEM_SPEC] * 3,
        scratch_shapes=in_vmem([kept_in[1], kept_in[2], kept_in[4]])
        + [pltpu.SemaphoreType.DMA((rows + 1,))],
        compiler_params=pltpu.CompilerParams(vmem_limit_bytes=40 << 20),
        cost_estimate=pl.CostEstimate(flops=8 * 10**9, bytes_accessed=2 * 10**7, transcendentals=0),
        name="push",
    )(wide, kept[0], in_hbm(kept[1]), in_hbm(kept[2]), *kept[3:])


def swapped_edges(low_edge, high_edge, axis):
    count = lax.axis_size(axis)
    odd = lax.axis_index(axis) % 2 == 1
    first = [(i, i ^ 1) for i in range(count)]
    second = [(i, ((i + 1) ^ 1) - 1) for i in range(1, count - 1)]
    to_first = jnp.where(odd, low_edge, high_edge)
    to_second = jnp.where(odd, high_edge, low_edge)
    from_first = lax.ppermute(to_first, axis, first)
    from_second = lax.ppermute(to_second, axis, second)
    low = jnp.where(odd, from_first, from_second)
    high = jnp.where(odd, from_second, from_first)
    return low, high


def with_halo(state):
    side = 2 * LANES
    low, high = swapped_edges(state[:, :, :side], state[:, :, -side:], ALONG_Y)
    state = jnp.concatenate([low, state, high], axis=2)
    low, high = swapped_edges(state[:2], state[-2:], "gx")
    return jnp.concatenate([low, state, high], axis=0)


def initial_state(position, velocity, volume):
    rows, _, cols, lanes = position.shape

    def body(position_ref, velocity_ref, volume_ref, state_out):
        blank = jnp.zeros((STATE_ROWS - 5, LANES), F32)
        for r in range(rows):
            volumes = volume_ref[r]
            size = jnp.exp(jnp.log(volumes) * (1.0 / 3.0))
            square = size * size
            size = size - (square * size - volumes) / (3.0 * square)
            for c in range(cols):
                row = slice(c, c + 1)
                new = [
                    position_ref[r, 0, row],
                    position_ref[r, 1, row],
                    velocity_ref[r, 0, row],
                    velocity_ref[r, 1, row],
                    size[row],
                    blank,
                ]
                state_out[r, :, c * LANES : (c + 1) * LANES] = jnp.concatenate(new, axis=0)

    return pl.pallas_call(
        body,
        out_shape=pltpu.VMEM((rows, STATE_ROWS, cols * lanes), F32),
        in_specs=[VMEM_SPEC] * 3,
        out_specs=VMEM_SPEC,
        name="initial",
    )(position, velocity, volume)


def on_device(
    fluid_position,
    fluid_velocity,
    fluid_volume,
    bound_offset,
    bound_cell,
    bound_body,
    body_state,
    mass_inverse,
    inertia_inverse,
):
    rows, cols = fluid_position.shape[0], fluid_position.shape[2]
    tile = Tile(rows, cols)
    shard_bodies = body_state.shape[1]
    owners = lax.axis_size("body")
    devices = lax.axis_size(EVERY)
    tiles_north = lax.axis_size(ALONG_Y)
    body_total = shard_bodies * owners
    own_bodies = body_total // devices
    sharing = devices // owners
    me = lax.axis_index(EVERY)

    state = initial_state(fluid_position, fluid_velocity, fluid_volume)
    shift = jnp.stack([lax.axis_index("gx") * rows, lax.axis_index(ALONG_Y) * cols])
    shift = shift.astype(F32)[:, None]
    slot = bound_body - me * own_bodies
    slot = jnp.where(slot < 0, slot + 2 * own_bodies, slot)

    bodies = jnp.concatenate([body_state, mass_inverse[None], inertia_inverse[None]], axis=0)
    by_home = bodies.reshape(7, sharing, own_bodies)
    place = lax.broadcasted_iota(jnp.int32, (1, sharing, 1), 1) % tiles_north
    after = jnp.concatenate([by_home[:, 1:], by_home[:, -1:]], axis=1)
    before = jnp.concatenate([by_home[:, :1], by_home[:, :-1]], axis=1)
    beside = jnp.where(place == tiles_north - 1, before, after)
    params = jnp.concatenate([by_home, beside], axis=2)
    params = jnp.transpose(params, (1, 0, 2)).reshape(sharing, 7 * 2 * own_bodies)
    params = jnp.concatenate([params] * owners, axis=0)

    for _ in range(SUBSTEPS - 1):
        state = run_substep(tile, with_halo(state))
    bound = (bound_offset, bound_cell, slot[None], shift)
    wide = with_halo(state)
    sums, *kept = run_bound(tile, wide, bound)

    partial = sums[:, :3].T.reshape(1, 6 * own_bodies)
    message = jnp.concatenate([jnp.broadcast_to(partial, (devices, 6 * own_bodies)), params], axis=1)
    received = lax.all_to_all(message, EVERY, 0, 0, tiled=True)
    position, velocity, depth = run_push(tile, wide, kept)
    partials = received[:, : 6 * own_bodies].reshape(devices, 3, 2 * own_bodies)
    partials = jnp.transpose(partials, (1, 0, 2))
    own_part, beside_part = partials[:, :, :own_bodies], partials[:, :, own_bodies:]
    place = lax.broadcasted_iota(jnp.int32, (1, devices, 1), 1) % tiles_north
    from_before = jnp.concatenate([beside_part[:, :1], beside_part[:, :-1]], axis=1)
    from_after = jnp.concatenate([beside_part[:, 1:], beside_part[:, -1:]], axis=1)
    totals = own_part + jnp.where(place > 0, from_before, 0.0)
    totals = totals + jnp.where(place == tiles_north - 2, from_after, 0.0)

    def integrate(state_of, mass_of, inertia_of, sums_of):
        span = step_time * SUBSTEPS
        east = state_of[2] + span * mass_of * sums_of[0]
        north = state_of[3] + span * mass_of * sums_of[1]
        torque = sums_of[2] - (state_of[0] * sums_of[1] - state_of[1] * sums_of[0])
        return jnp.stack([east, north, state_of[4] + span * inertia_of * torque])

    shard = lax.axis_index("body")
    shard_sums = lax.dynamic_slice_in_dim(totals, shard * sharing, sharing, axis=1)
    shard_sums = shard_sums.reshape(3, shard_bodies)
    motion = integrate(body_state, mass_inverse, inertia_inverse, shard_sums)

    tile_place = lax.axis_index(ALONG_Y)
    other = jnp.where(tile_place == tiles_north - 1, me - 1, me + 1)
    mine = lax.dynamic_slice_in_dim(totals, me, 1, axis=1)[:, 0]
    theirs = lax.dynamic_slice_in_dim(totals, other, 1, axis=1)[:, 0]
    local_sums = jnp.concatenate([mine, theirs], axis=1)
    local = lax.dynamic_slice_in_dim(received, me // sharing, 1, axis=0)[0, 6 * own_bodies :]
    local = local.reshape(7, 2 * own_bodies)
    local_motion = integrate(local[:5], local[5], local[6], local_sums)
    table = jnp.concatenate([local_motion, local[:2]], axis=0)
    chosen = slot[None, :, None] == jnp.arange(2 * own_bodies, dtype=jnp.int32)
    picked = jnp.sum(jnp.where(chosen, table[:, None, :], 0.0), axis=-1)
    place_east = bound_cell[0].astype(F32) + bound_offset[0]
    place_north = bound_cell[1].astype(F32) + bound_offset[1]
    bound_velocity = jnp.stack(
        [
            picked[0] - picked[2] * (place_north - picked[4]),
            picked[1] + picked[2] * (place_east - picked[3]),
        ]
    )
    return position, velocity, depth, motion, bound_velocity


def solution(mesh):
    return jax.shard_map(
        on_device,
        mesh=mesh,
        in_specs=(
            P("gx", None, ("gy", "body"), None),
            P("gx", None, ("gy", "body"), None),
            P("gx", ("gy", "body"), None),
            P(None, ("gx", "gy", "body")),
            P(None, ("gx", "gy", "body")),
            P(("gx", "gy", "body")),
            P(None, "body"),
            P("body"),
            P("body"),
        ),
        out_specs=(
            P("gx", None, ("gy", "body"), None),
            P("gx", None, ("gy", "body"), None),
            P("gx", ("gy", "body"), None),
            P(None, "body"),
            P(None, ("gx", "gy", "body")),
        ),
        check_vma=False,
    )
```

```python
import jax
import jax.numpy as jnp
from jax import lax
from jax.experimental import pallas as pl
from jax.experimental.pallas import tpu as pltpu
from jax.sharding import PartitionSpec as P

SUBSTEPS = 3

gravity = 3.0
viscosity = 1.0
step_time = 0.05

ALONG_Y = ("gy", "body")
EVERY = ("gx", "gy", "body")
LANES = 128
GROUP = 128
FAR = 4096.0
F32 = jnp.float32
BF16 = jnp.bfloat16

STATE_ROWS = 8


def pieces(values):
    high = values.astype(BF16).astype(F32)
    rest = values - high
    middle = rest.astype(BF16).astype(F32)
    low = (rest - middle).astype(BF16).astype(F32)
    return high, middle, low


def near_rows(parts):
    high, middle, low = parts
    return [high, middle, low, high, middle, high]


def own_rows(parts):
    high, middle, low = parts
    return [high, high, high, middle, middle, low]


def row_iota(rows, lanes):
    return lax.broadcasted_iota(jnp.int32, (rows, lanes), 0)


def across(rows, pairs):
    dims = (((1,), (1,)), ((), ()))
    return lax.dot_general(rows, pairs, dims, preferred_element_type=F32)


def lane_sums(values):
    return jnp.sum(values.T, axis=0, keepdims=True)


class Tile:
    def __init__(self, rows, cols):
        self.rows, self.cols = rows, cols
        self.wide_rows, self.wide_cols = rows + 4, cols + 4
        self.ring_rows, self.ring_cols = rows + 2, cols + 2
        self.mask_rows = self.ring_rows + self.ring_cols
        self.depth = -(-(24 + self.mask_rows) // 16) * 16
        self.east_centre = float(self.wide_rows // 2)
        self.north_centre = float(self.wide_cols // 2)


def lane_block(ref_lanes):
    return lax.broadcasted_iota(jnp.int32, (1, ref_lanes), 1) // LANES


def depth_half(tile, wide_ref, bound_refs, kept, scratch):
    with_bound = bound_refs is not None
    if with_bound:
        (place_ref, cell_ref, slot_ref, shift_ref, sums_out, back_ref, total_ref, exact_ref) = bound_refs[:8]
        place_all, cell_all, pair_all, side_all, copies = bound_refs[8:]
        place_copy = pltpu.make_async_copy(place_all, place_ref, copies.at[0])
        cell_copy = pltpu.make_async_copy(cell_all, cell_ref, copies.at[1])
        place_copy.start()
        cell_copy.start()
    depth_ref, pair_ref, side_ref, heavy_ref, sums_ref = kept
    near_ref, own_ref, drag_ref = scratch
    rows, cols = tile.rows, tile.cols
    wide_lanes = tile.wide_cols * LANES
    ring_lanes = tile.ring_cols * LANES

    block_of = lane_block(wide_lanes)
    north_of = block_of.astype(F32) - tile.north_centre

    def place_of(r):
        state = wide_ref[r]
        east_shift = jnp.asarray(r, F32) - tile.east_centre
        return state[0:1] + east_shift, state[1:2] + north_of, state

    def feature_row(r, carry):
        east, north, state = place_of(r)
        size = state[4:5]
        reach = east * east + north * north
        near = jnp.concatenate([size, size * east, size * north, -(size * reach)], axis=0)
        near = jnp.concatenate(near_rows(pieces(near)), axis=0)
        extra = tile.depth - 24
        which = row_iota(extra, wide_lanes)
        is_row = which == r - 1
        is_col = which - tile.ring_rows == jnp.broadcast_to(block_of, (extra, wide_lanes)) - 1
        flags = jnp.where(is_row | is_col, jnp.broadcast_to(size, (extra, wide_lanes)), 0.0)
        near_ref[r] = jnp.concatenate([near, flags], axis=0).astype(BF16)
        return carry

    lax.fori_loop(0, tile.wide_rows, feature_row, 0, unroll=8)

    def own_features(east, north):
        reach = 1.0 - east * east - north * north
        own = jnp.concatenate([reach, 2.0 * east, 2.0 * north, jnp.ones_like(east)], axis=0)
        return jnp.concatenate(own_rows(pieces(own)), axis=0)

    def own_row(r, carry):
        east, north, state = place_of(r)
        own = own_features(east, north)
        own = jnp.concatenate([own, jnp.zeros((8, wide_lanes), F32)], axis=0)
        for c in range(tile.ring_cols):
            part = own[:, (c + 1) * LANES : (c + 2) * LANES]
            own_ref[r - 1, c] = part.T.astype(BF16)
        high, middle, _ = pieces(state[2:4, LANES : LANES + ring_lanes])
        ones = jnp.ones((1, ring_lanes), F32)
        blank = jnp.zeros((6, ring_lanes), F32)
        speeds = jnp.concatenate([high, ones, blank[:5], middle, blank], axis=0)
        drag_ref[r - 1] = speeds.astype(BF16)
        return carry

    lax.fori_loop(1, tile.ring_rows + 1, own_row, 0, unroll=6)

    def store_pieces(ref, index, place, places, values):
        high = values.astype(BF16)
        low = (values - high.astype(F32)).astype(BF16)
        ref[index, :, place * LANES : (place + 1) * LANES] = high
        ref[index, :, (places + place) * LANES : (places + place + 1) * LANES] = low

    def depth_block(r, c, keep, side=None):
        own = own_ref[r - 1, c - 1]
        lanes = pl.ds(pl.multiple_of((c - 1) * LANES, LANES), 3 * LANES)
        near = jnp.concatenate([near_ref[r + e - 1, 0:32, lanes] for e in range(3)], axis=1)
        all_close = jnp.maximum(jnp.dot(own, near, preferred_element_type=F32), 0.0)
        total = jnp.zeros((LANES, LANES), F32)
        thirds = []
        for block in range(9):
            close = all_close[:, block * LANES : (block + 1) * LANES]
            second = close * close
            third = second * close
            total = total + third
            if keep is not None:
                thirds.append(third.astype(BF16))
                store_pieces(pair_ref, keep, block, 9, second)
            elif block in side[1]:
                store_pieces(side_ref, side[0], side[1].index(block), 3, second)
        depth = lane_sums(total) * (1.0 / LANES)
        depth_ref[r - 1, 0:1, pl.ds(pl.multiple_of((c - 1) * LANES, LANES), LANES)] = depth
        if keep is not None:
            lanes = pl.ds(pl.multiple_of((c - 2) * LANES, LANES), 3 * LANES)
            speeds = jnp.concatenate([drag_ref[r + e - 2, :, lanes] for e in range(3)], axis=1)
            drag = across(speeds, jnp.concatenate(thirds, axis=1))
            lanes = pl.ds(pl.multiple_of((c - 2) * LANES, LANES), LANES)
            sums_ref[r - 2, 8:16, lanes] = drag[0:8] + drag[8:16]

    def own_depth(k, carry):
        depth_block(k // cols + 2, k % cols + 2, k)
        return carry

    lax.fori_loop(0, rows * cols, own_depth, 0, unroll=32)

    if with_bound:
        pair_copy = pltpu.make_async_copy(pair_ref, pair_all, copies.at[2])
        pair_copy.start()

    def side_depth(c, carry):
        depth_block(1, 1 + c, None, (c, (6, 7, 8)))
        depth_block(rows + 2, 1 + c, None, (tile.ring_cols + c, (0, 1, 2)))
        return carry

    lax.fori_loop(0, tile.ring_cols, side_depth, 0, unroll=10)

    def end_depth(k, carry):
        depth_block(2 + k, 1, None, (2 * tile.ring_cols + k, (2, 5, 8)))
        depth_block(2 + k, cols + 2, None, (2 * tile.ring_cols + rows + k, (0, 3, 6)))
        return carry

    lax.fori_loop(0, rows, end_depth, 0, unroll=4)

    if with_bound:
        side_copy = pltpu.make_async_copy(side_ref, side_all, copies.at[3])
        side_copy.start()

    def column_row(r, carry):
        east, north, state = place_of(r)
        inner = slice(LANES, LANES + ring_lanes)
        east, north, state = east[:, inner], north[:, inner], state[:, inner]
        size = state[4:5]
        deep = size * depth_ref[r - 1, 0:1]
        blank = jnp.zeros((2, ring_lanes), F32)
        first = [size, deep, size * east, size * north, deep * east, deep * north, blank]
        first = jnp.concatenate(first, axis=0)
        if with_bound:
            exact_ref[r - 1] = first
        heavy = pieces(first * (size * size))
        heavy_ref[r - 1] = jnp.concatenate(heavy, axis=0).astype(BF16)
        return carry

    lax.fori_loop(1, tile.ring_rows + 1, column_row, 0, unroll=6)

    if with_bound:
        place_copy.wait()
        cell_copy.wait()
        groups = place_ref.shape[1] // GROUP
        cell = cell_ref[...]
        local = cell.astype(F32) - shift_ref[...]
        east = place_ref[0:1] + (local[0:1] + (2.0 - tile.east_centre))
        north = place_ref[1:2] + (local[1:2] + (2.0 - tile.north_centre))
        lanes = place_ref.shape[1]
        extra = tile.depth - 24
        which = row_iota(extra, lanes).astype(F32)
        apart_row = jnp.abs(which - (local[0:1] + 1.0))
        apart_col = jnp.abs(which - tile.ring_rows - (local[1:2] + 1.0))
        apart = jnp.where(which < tile.ring_rows - 0.5, apart_row, apart_col)
        apart = jnp.where(which < tile.mask_rows - 0.5, apart, 0.0)
        masks = jnp.where(apart > 1.5, -FAR, 0.0)
        bound = jnp.concatenate([own_features(east, north), masks], axis=0)
        for group in range(groups):
            back_ref[group] = bound[:, group * GROUP : (group + 1) * GROUP].T.astype(BF16)

        def bound_group(group, carry):
            own = back_ref[group]
            totals = [jnp.zeros((GROUP, LANES), F32) for _ in range(3)]
            for r in range(tile.ring_rows):
                near = near_ref[r + 1, :, LANES : LANES + ring_lanes]
                close = jnp.maximum(jnp.dot(own, near, preferred_element_type=F32), 0.0)
                for c in range(tile.ring_cols):
                    lanes = slice(c * LANES, (c + 1) * LANES)
                    second = close[:, lanes] * close[:, lanes]
                    for which, row in enumerate((1, 4, 5)):
                        weight = exact_ref[r, row : row + 1, lanes]
                        totals[which] = totals[which] + second * weight
            for which in range(3):
                total_ref[which, pl.ds(pl.multiple_of(group * GROUP, GROUP), GROUP)] = totals[which]
            return carry

        lax.fori_loop(0, groups, bound_group, 0)
        merged = []
        for which in range(3):
            parts = []
            for group in range(lanes // LANES):
                parts.append(lane_sums(total_ref[which, group * LANES : (group + 1) * LANES]))
            merged.append(jnp.concatenate(parts, axis=1))
        factor = 6.0 * gravity / LANES
        force_east = factor * (east * merged[0] - merged[1])
        force_north = factor * (north * merged[0] - merged[2])
        cell_place = cell.astype(F32)
        torque = (cell_place[0:1] + place_ref[0:1]) * force_north
        torque = torque - (cell_place[1:2] + place_ref[1:2]) * force_east
        chosen = row_iota(8, lanes) == slot_ref[...]
        columns = []
        for values in (force_east, force_north, torque):
            picked = jnp.where(chosen, jnp.broadcast_to(values, (8, lanes)), 0.0)
            columns.append(jnp.sum(picked, axis=1, keepdims=True))
        lane = lax.broadcasted_iota(jnp.int32, (8, LANES), 1)
        result = jnp.where(lane == 0, columns[0], jnp.where(lane == 1, columns[1], columns[2]))
        sums_out[...] = result
        pair_copy.wait()
        side_copy.wait()


def push_half(tile, wide_ref, kept, state_out, final_out=None, row_copy=None):
    depth_ref, pair_ref, side_ref, heavy_ref, sums_ref = kept
    rows, cols = tile.rows, tile.cols
    north_of = lane_block(tile.wide_cols * LANES).astype(F32) - tile.north_centre

    def place_of(r):
        state = wide_ref[r]
        east_shift = jnp.asarray(r, F32) - tile.east_centre
        return state[0:1] + east_shift, state[1:2] + north_of, state

    def weights_from(r, c, e, f):
        from_row, from_col = r + e, c + f
        if 1 <= from_row <= rows and 1 <= from_col <= cols:
            ref, index = pair_ref, (from_row - 1) * cols + from_col - 1
            place, places = (2 - e) * 3 + 2 - f, 9
        elif from_row in (0, rows + 1):
            ref, index = side_ref, from_col + (tile.ring_cols if from_row else 0)
            place, places = 2 - f, 3
        else:
            ref, index = side_ref, 2 * tile.ring_cols + from_row - 1 + (rows if from_col else 0)
            place, places = 2 - e, 3
        high = ref[index, :, place * LANES : (place + 1) * LANES]
        low = ref[index, :, (places + place) * LANES : (places + place + 1) * LANES]
        return high, low

    def push_block(r, c):
        lanes = slice(c * LANES, (c + 3) * LANES)
        near = [heavy_ref[r + e, :, lanes] for e in range(3)]
        highs, lows = zip(*[weights_from(r, c, e, f) for e in range(3) for f in range(3)])
        weights = jnp.concatenate(highs + lows, axis=0)
        total = jnp.dot(jnp.concatenate(near + near, axis=1), weights, preferred_element_type=F32)
        merged = total[0:8] + total[8:16] + total[16:24]
        sums_ref[r, 0:8, c * LANES : (c + 1) * LANES] = merged

    for r in range(rows):
        if final_out is not None:
            for step in {0: range(min(2, rows) + 1), rows - 1: ()}.get(r, (r + 2,)):
                row_copy(step).wait()
        for c in range(cols):
            push_block(r, c)

    def update_row(r, carry):
        east, north, state = place_of(r + 2)
        inner = slice(2 * LANES, (2 + cols) * LANES)
        east, north, state = east[:, inner], north[:, inner], state[:, inner]
        drag = sums_ref[r, 8:16]
        sums = sums_ref[r, 0:8] / (state[4:5] * state[4:5])
        depth = depth_ref[r + 1, 0:1, LANES : (1 + cols) * LANES]
        speed_east, speed_north = state[2:3], state[3:4]
        heavy = depth * sums[0:1] + sums[1:2]
        push_east = heavy * east - depth * sums[2:3] - sums[4:5]
        push_north = heavy * north - depth * sums[3:4] - sums[5:6]
        drag_east = drag[0:1] - speed_east * drag[2:3]
        drag_north = drag[1:2] - speed_north * drag[2:3]
        scale = 3.0 * gravity / LANES
        thin = viscosity / LANES
        speed_east = speed_east + step_time * (scale * push_east + thin * drag_east)
        speed_north = speed_north + step_time * (scale * push_north + thin * drag_north)
        east = state[0:1] + step_time * speed_east
        north = state[1:2] + step_time * speed_north
        if state_out is not None:
            blank = jnp.zeros((STATE_ROWS - 5, cols * LANES), F32)
            new = [east, north, speed_east, speed_north, state[4:5], blank]
            state_out[r] = jnp.concatenate(new, axis=0)
        else:
            position_out, velocity_out, depth_out = final_out
            for c in range(cols):
                lanes = slice(c * LANES, (c + 1) * LANES)
                position_out[r, 0, c : c + 1] = east[:, lanes]
                position_out[r, 1, c : c + 1] = north[:, lanes]
                velocity_out[r, 0, c : c + 1] = speed_east[:, lanes]
                velocity_out[r, 1, c : c + 1] = speed_north[:, lanes]
                depth_out[r, c : c + 1] = depth[:, lanes]
        return carry

    lax.fori_loop(0, rows, update_row, 0, unroll=4)


def kept_shapes(tile):
    rows, cols = tile.rows, tile.cols
    return [
        ((tile.ring_rows, 8, tile.ring_cols * LANES), F32),
        ((rows * cols, LANES, 18 * LANES), BF16),
        ((2 * (tile.ring_cols + rows), LANES, 6 * LANES), BF16),
        ((tile.ring_rows, 24, tile.ring_cols * LANES), BF16),
        ((rows, 16, cols * LANES), F32),
    ]


def scratch_shapes(tile):
    return [
        ((tile.wide_rows, tile.depth, tile.wide_cols * LANES), BF16),
        ((tile.ring_rows, tile.ring_cols, LANES, 32), BF16),
        ((tile.ring_rows, 16, tile.ring_cols * LANES), BF16),
    ]


def in_vmem(shapes):
    return [pltpu.VMEM(shape, dtype) for shape, dtype in shapes]


VMEM_SPEC = pl.BlockSpec(memory_space=pltpu.VMEM)
LIMIT = 52 << 20


def run_substep(tile, wide):
    def body(wide_ref, state_out, *refs):
        kept, scratch = refs[:5], refs[5:]
        depth_half(tile, wide_ref, None, kept, scratch)
        push_half(tile, wide_ref, kept, state_out)

    return pl.pallas_call(
        body,
        out_shape=jax.ShapeDtypeStruct((tile.rows, STATE_ROWS, tile.cols * LANES), F32),
        in_specs=[VMEM_SPEC],
        out_specs=VMEM_SPEC,
        scratch_shapes=in_vmem(kept_shapes(tile) + scratch_shapes(tile)),
        compiler_params=pltpu.CompilerParams(vmem_limit_bytes=LIMIT),
        name="substep",
    )(wide)


HBM_SPEC = pl.BlockSpec(memory_space=pltpu.HBM)


def in_hbm(array):
    return pltpu.with_memory_space_constraint(array, pltpu.HBM)


def run_bound(tile, wide, bound):
    place, cell, slot, shift = bound
    lanes = place.shape[1]
    back = [
        ((lanes // GROUP, GROUP, tile.depth), BF16),
        ((3, lanes, LANES), F32),
        ((tile.ring_rows, 8, tile.ring_cols * LANES), F32),
        (place.shape, F32),
        (cell.shape, jnp.int32),
    ]
    depth_shape, pair_shape, side_shape, heavy_shape, sums_shape = kept_shapes(tile)

    def body(wide_ref, place_all, cell_all, slot_ref, shift_ref, sums_out, *refs):
        depth_ref, pair_all, side_all, heavy_ref, sums_ref, pair_ref, side_ref = refs[:7]
        scratch, back_refs, copies = refs[7:10], refs[10:15], refs[15]
        bound_refs = back_refs[3:] + (slot_ref, shift_ref, sums_out) + back_refs[:3]
        bound_refs = bound_refs + (place_all, cell_all, pair_all, side_all, copies)
        kept_refs = (depth_ref, pair_ref, side_ref, heavy_ref, sums_ref)
        depth_half(tile, wide_ref, bound_refs, kept_refs, scratch)

    outs = [((8, LANES), F32), depth_shape, pair_shape, side_shape, heavy_shape, sums_shape]
    return pl.pallas_call(
        body,
        out_shape=[jax.ShapeDtypeStruct(shape, dtype) for shape, dtype in outs],
        in_specs=[VMEM_SPEC, HBM_SPEC, HBM_SPEC, VMEM_SPEC, VMEM_SPEC],
        out_specs=[VMEM_SPEC, VMEM_SPEC, HBM_SPEC, HBM_SPEC, VMEM_SPEC, VMEM_SPEC],
        scratch_shapes=in_vmem([pair_shape, side_shape] + scratch_shapes(tile) + back)
        + [pltpu.SemaphoreType.DMA((4,))],
        compiler_params=pltpu.CompilerParams(vmem_limit_bytes=LIMIT),
        name="depth_bound",
    )(wide, in_hbm(place), in_hbm(cell), slot, shift)


def run_push(tile, wide, kept):
    rows, cols = tile.rows, tile.cols
    pair = jax.ShapeDtypeStruct((rows, 2, cols, LANES), F32)
    kept_in = kept_shapes(tile)

    def body(wide_ref, depth_ref, pair_all, side_all, heavy_ref, drag_sums, *refs):
        position, velocity, depth, pair_ref, side_ref, sums_ref, copies = refs

        def row_copy(step):
            if step == 0:
                return pltpu.make_async_copy(side_all, side_ref, copies.at[0])
            part = pl.ds((step - 1) * cols, cols)
            return pltpu.make_async_copy(pair_all.at[part], pair_ref.at[part], copies.at[step])

        for step in range(rows + 1):
            row_copy(step).start()
        sums_ref[...] = drag_sums[...]
        kept_refs = (depth_ref, pair_ref, side_ref, heavy_ref, sums_ref)
        push_half(tile, wide_ref, kept_refs, None, (position, velocity, depth), row_copy)

    return pl.pallas_call(
        body,
        out_shape=[pair, pair, jax.ShapeDtypeStruct((rows, cols, LANES), F32)],
        in_specs=[VMEM_SPEC, VMEM_SPEC, HBM_SPEC, HBM_SPEC, VMEM_SPEC, VMEM_SPEC],
        out_specs=[VMEM_SPEC] * 3,
        scratch_shapes=in_vmem([kept_in[1], kept_in[2], kept_in[4]])
        + [pltpu.SemaphoreType.DMA((rows + 1,))],
        compiler_params=pltpu.CompilerParams(vmem_limit_bytes=40 << 20),
        cost_estimate=pl.CostEstimate(flops=8 * 10**9, bytes_accessed=2 * 10**7, transcendentals=0),
        name="push",
    )(wide, kept[0], in_hbm(kept[1]), in_hbm(kept[2]), *kept[3:])


def swapped_edges(low_edge, high_edge, axis):
    count = lax.axis_size(axis)
    odd = lax.axis_index(axis) % 2 == 1
    first = [(i, i ^ 1) for i in range(count)]
    second = [(i, ((i + 1) ^ 1) - 1) for i in range(1, count - 1)]
    to_first = jnp.where(odd, low_edge, high_edge)
    to_second = jnp.where(odd, high_edge, low_edge)
    from_first = lax.ppermute(to_first, axis, first)
    from_second = lax.ppermute(to_second, axis, second)
    low = jnp.where(odd, from_first, from_second)
    high = jnp.where(odd, from_second, from_first)
    return low, high


def with_halo(state):
    side = 2 * LANES
    low, high = swapped_edges(state[:, :, :side], state[:, :, -side:], ALONG_Y)
    state = jnp.concatenate([low, state, high], axis=2)
    low, high = swapped_edges(state[:2], state[-2:], "gx")
    return jnp.concatenate([low, state, high], axis=0)


def initial_state(position, velocity, volume):
    rows, _, cols, lanes = position.shape

    def body(position_ref, velocity_ref, volume_ref, state_out):
        blank = jnp.zeros((STATE_ROWS - 5, LANES), F32)
        for r in range(rows):
            volumes = volume_ref[r]
            size = jnp.exp(jnp.log(volumes) * (1.0 / 3.0))
            square = size * size
            size = size - (square * size - volumes) / (3.0 * square)
            for c in range(cols):
                row = slice(c, c + 1)
                new = [
                    position_ref[r, 0, row],
                    position_ref[r, 1, row],
                    velocity_ref[r, 0, row],
                    velocity_ref[r, 1, row],
                    size[row],
                    blank,
                ]
                state_out[r, :, c * LANES : (c + 1) * LANES] = jnp.concatenate(new, axis=0)

    return pl.pallas_call(
        body,
        out_shape=pltpu.VMEM((rows, STATE_ROWS, cols * lanes), F32),
        in_specs=[VMEM_SPEC] * 3,
        out_specs=VMEM_SPEC,
        name="initial",
    )(position, velocity, volume)


def on_device(
    fluid_position,
    fluid_velocity,
    fluid_volume,
    bound_offset,
    bound_cell,
    bound_body,
    body_state,
    mass_inverse,
    inertia_inverse,
):
    rows, cols = fluid_position.shape[0], fluid_position.shape[2]
    tile = Tile(rows, cols)
    shard_bodies = body_state.shape[1]
    owners = lax.axis_size("body")
    devices = lax.axis_size(EVERY)
    tiles_north = lax.axis_size(ALONG_Y)
    body_total = shard_bodies * owners
    own_bodies = body_total // devices
    sharing = devices // owners
    me = lax.axis_index(EVERY)

    state = initial_state(fluid_position, fluid_velocity, fluid_volume)
    shift = jnp.stack([lax.axis_index("gx") * rows, lax.axis_index(ALONG_Y) * cols])
    shift = shift.astype(F32)[:, None]
    slot = bound_body - me * own_bodies
    slot = jnp.where(slot < 0, slot + 2 * own_bodies, slot)

    bodies = jnp.concatenate([body_state, mass_inverse[None], inertia_inverse[None]], axis=0)
    by_home = bodies.reshape(7, sharing, own_bodies)
    place = lax.broadcasted_iota(jnp.int32, (1, sharing, 1), 1) % tiles_north
    after = jnp.concatenate([by_home[:, 1:], by_home[:, -1:]], axis=1)
    before = jnp.concatenate([by_home[:, :1], by_home[:, :-1]], axis=1)
    beside = jnp.where(place == tiles_north - 1, before, after)
    params = jnp.concatenate([by_home, beside], axis=2)
    params = jnp.transpose(params, (1, 0, 2)).reshape(sharing, 7 * 2 * own_bodies)
    params = jnp.concatenate([params] * owners, axis=0)

    for _ in range(SUBSTEPS - 1):
        state = run_substep(tile, with_halo(state))
    bound = (bound_offset, bound_cell, slot[None], shift)
    wide = with_halo(state)
    sums, *kept = run_bound(tile, wide, bound)

    partial = sums[:, :3].T.reshape(1, 6 * own_bodies)
    message = jnp.concatenate([jnp.broadcast_to(partial, (devices, 6 * own_bodies)), params], axis=1)
    received = lax.all_to_all(message, EVERY, 0, 0, tiled=True)
    position, velocity, depth = run_push(tile, wide, kept)
    partials = received[:, : 6 * own_bodies].reshape(devices, 3, 2 * own_bodies)
    partials = jnp.transpose(partials, (1, 0, 2))
    own_part, beside_part = partials[:, :, :own_bodies], partials[:, :, own_bodies:]
    place = lax.broadcasted_iota(jnp.int32, (1, devices, 1), 1) % tiles_north
    from_before = jnp.concatenate([beside_part[:, :1], beside_part[:, :-1]], axis=1)
    from_after = jnp.concatenate([beside_part[:, 1:], beside_part[:, -1:]], axis=1)
    totals = own_part + jnp.where(place > 0, from_before, 0.0)
    totals = totals + jnp.where(place == tiles_north - 2, from_after, 0.0)

    def integrate(state_of, mass_of, inertia_of, sums_of):
        span = step_time * SUBSTEPS
        east = state_of[2] + span * mass_of * sums_of[0]
        north = state_of[3] + span * mass_of * sums_of[1]
        torque = sums_of[2] - (state_of[0] * sums_of[1] - state_of[1] * sums_of[0])
        return jnp.stack([east, north, state_of[4] + span * inertia_of * torque])

    shard = lax.axis_index("body")
    shard_sums = lax.dynamic_slice_in_dim(totals, shard * sharing, sharing, axis=1)
    shard_sums = shard_sums.reshape(3, shard_bodies)
    motion = integrate(body_state, mass_inverse, inertia_inverse, shard_sums)

    tile_place = lax.axis_index(ALONG_Y)
    other = jnp.where(tile_place == tiles_north - 1, me - 1, me + 1)
    mine = lax.dynamic_slice_in_dim(totals, me, 1, axis=1)[:, 0]
    theirs = lax.dynamic_slice_in_dim(totals, other, 1, axis=1)[:, 0]
    local_sums = jnp.concatenate([mine, theirs], axis=1)
    local = lax.dynamic_slice_in_dim(received, me // sharing, 1, axis=0)[0, 6 * own_bodies :]
    local = local.reshape(7, 2 * own_bodies)
    local_motion = integrate(local[:5], local[5], local[6], local_sums)
    table = jnp.concatenate([local_motion, local[:2]], axis=0)
    chosen = slot[None, :, None] == jnp.arange(2 * own_bodies, dtype=jnp.int32)
    picked = jnp.sum(jnp.where(chosen, table[:, None, :], 0.0), axis=-1)
    place_east = bound_cell[0].astype(F32) + bound_offset[0]
    place_north = bound_cell[1].astype(F32) + bound_offset[1]
    bound_velocity = jnp.stack(
        [
            picked[0] - picked[2] * (place_north - picked[4]),
            picked[1] + picked[2] * (place_east - picked[3]),
        ]
    )
    return position, velocity, depth, motion, bound_velocity


def solution(mesh):
    return jax.shard_map(
        on_device,
        mesh=mesh,
        in_specs=(
            P("gx", None, ("gy", "body"), None),
            P("gx", None, ("gy", "body"), None),
            P("gx", ("gy", "body"), None),
            P(None, ("gx", "gy", "body")),
            P(None, ("gx", "gy", "body")),
            P(("gx", "gy", "body")),
            P(None, "body"),
            P("body"),
            P("body"),
        ),
        out_specs=(
            P("gx", None, ("gy", "body"), None),
            P("gx", None, ("gy", "body"), None),
            P("gx", ("gy", "body"), None),
            P(None, "body"),
            P(None, ("gx", "gy", "body")),
        ),
        check_vma=False,
    )
```

```python
import jax
import jax.numpy as jnp
from jax import lax
from jax.experimental import pallas as pl
from jax.experimental.pallas import tpu as pltpu
from jax.sharding import PartitionSpec as P

SUBSTEPS = 3

gravity = 3.0
viscosity = 1.0
step_time = 0.05

ALONG_Y = ("gy", "body")
EVERY = ("gx", "gy", "body")
LANES = 128
GROUP = 128
FAR = 4096.0
F32 = jnp.float32
BF16 = jnp.bfloat16

STATE_ROWS = 8


def pieces(values):
    high = values.astype(BF16).astype(F32)
    rest = values - high
    middle = rest.astype(BF16).astype(F32)
    low = (rest - middle).astype(BF16).astype(F32)
    return high, middle, low


def near_rows(parts):
    high, middle, low = parts
    return [high, middle, low, high, middle, high]


def own_rows(parts):
    high, middle, low = parts
    return [high, high, high, middle, middle, low]


def row_iota(rows, lanes):
    return lax.broadcasted_iota(jnp.int32, (rows, lanes), 0)


def across(rows, pairs):
    dims = (((1,), (1,)), ((), ()))
    return lax.dot_general(rows, pairs, dims, preferred_element_type=F32)


def lane_sums(values):
    return jnp.sum(values.T, axis=0, keepdims=True)


class Tile:
    def __init__(self, rows, cols):
        self.rows, self.cols = rows, cols
        self.wide_rows, self.wide_cols = rows + 4, cols + 4
        self.ring_rows, self.ring_cols = rows + 2, cols + 2
        self.mask_rows = self.ring_rows + self.ring_cols
        self.depth = -(-(24 + self.mask_rows) // 16) * 16
        self.east_centre = float(self.wide_rows // 2)
        self.north_centre = float(self.wide_cols // 2)


def lane_block(ref_lanes):
    return lax.broadcasted_iota(jnp.int32, (1, ref_lanes), 1) // LANES


def depth_half(tile, wide_ref, bound_refs, kept, scratch):
    with_bound = bound_refs is not None
    if with_bound:
        (place_ref, cell_ref, slot_ref, shift_ref, sums_out, back_ref, total_ref, exact_ref) = bound_refs[:8]
        place_all, cell_all, pair_all, side_all, copies = bound_refs[8:]
        place_copy = pltpu.make_async_copy(place_all, place_ref, copies.at[0])
        cell_copy = pltpu.make_async_copy(cell_all, cell_ref, copies.at[1])
        place_copy.start()
        cell_copy.start()
    depth_ref, pair_ref, side_ref, heavy_ref, sums_ref = kept
    near_ref, own_ref, drag_ref = scratch
    rows, cols = tile.rows, tile.cols
    wide_lanes = tile.wide_cols * LANES
    ring_lanes = tile.ring_cols * LANES

    block_of = lane_block(wide_lanes)
    north_of = block_of.astype(F32) - tile.north_centre

    def place_of(r):
        state = wide_ref[r]
        east_shift = jnp.asarray(r, F32) - tile.east_centre
        return state[0:1] + east_shift, state[1:2] + north_of, state

    def feature_row(r, carry):
        east, north, state = place_of(r)
        size = state[4:5]
        reach = east * east + north * north
        near = jnp.concatenate([size, size * east, size * north, -(size * reach)], axis=0)
        near = jnp.concatenate(near_rows(pieces(near)), axis=0)
        extra = tile.depth - 24
        which = row_iota(extra, wide_lanes)
        is_row = which == r - 1
        is_col = which - tile.ring_rows == jnp.broadcast_to(block_of, (extra, wide_lanes)) - 1
        flags = jnp.where(is_row | is_col, jnp.broadcast_to(size, (extra, wide_lanes)), 0.0)
        near_ref[r] = jnp.concatenate([near, flags], axis=0).astype(BF16)
        return carry

    lax.fori_loop(0, tile.wide_rows, feature_row, 0, unroll=8)

    def own_features(east, north):
        reach = 1.0 - east * east - north * north
        own = jnp.concatenate([reach, 2.0 * east, 2.0 * north, jnp.ones_like(east)], axis=0)
        return jnp.concatenate(own_rows(pieces(own)), axis=0)

    def own_row(r, carry):
        east, north, state = place_of(r)
        own = own_features(east, north)
        own = jnp.concatenate([own, jnp.zeros((8, wide_lanes), F32)], axis=0)
        for c in range(tile.ring_cols):
            part = own[:, (c + 1) * LANES : (c + 2) * LANES]
            own_ref[r - 1, c] = part.T.astype(BF16)
        high, middle, _ = pieces(state[2:4, LANES : LANES + ring_lanes])
        ones = jnp.ones((1, ring_lanes), F32)
        blank = jnp.zeros((6, ring_lanes), F32)
        speeds = jnp.concatenate([high, ones, blank[:5], middle, blank], axis=0)
        drag_ref[r - 1] = speeds.astype(BF16)
        return carry

    lax.fori_loop(1, tile.ring_rows + 1, own_row, 0, unroll=6)

    def store_pieces(ref, index, place, places, values):
        high = values.astype(BF16)
        low = (values - high.astype(F32)).astype(BF16)
        ref[index, :, place * LANES : (place + 1) * LANES] = high
        ref[index, :, (places + place) * LANES : (places + place + 1) * LANES] = low

    def depth_block(r, c, keep, side=None):
        own = own_ref[r - 1, c - 1]
        lanes = pl.ds(pl.multiple_of((c - 1) * LANES, LANES), 3 * LANES)
        near = jnp.concatenate([near_ref[r + e - 1, 0:32, lanes] for e in range(3)], axis=1)
        all_close = jnp.maximum(jnp.dot(own, near, preferred_element_type=F32), 0.0)
        total = jnp.zeros((LANES, LANES), F32)
        thirds = []
        for block in range(9):
            close = all_close[:, block * LANES : (block + 1) * LANES]
            second = close * close
            third = second * close
            total = total + third
            if keep is not None:
                thirds.append(third.astype(BF16))
                store_pieces(pair_ref, keep, block, 9, second)
            elif block in side[1]:
                store_pieces(side_ref, side[0], side[1].index(block), 3, second)
        depth = lane_sums(total) * (1.0 / LANES)
        depth_ref[r - 1, 0:1, pl.ds(pl.multiple_of((c - 1) * LANES, LANES), LANES)] = depth
        if keep is not None:
            lanes = pl.ds(pl.multiple_of((c - 2) * LANES, LANES), 3 * LANES)
            speeds = jnp.concatenate([drag_ref[r + e - 2, :, lanes] for e in range(3)], axis=1)
            drag = across(speeds, jnp.concatenate(thirds, axis=1))
            lanes = pl.ds(pl.multiple_of((c - 2) * LANES, LANES), LANES)
            sums_ref[r - 2, 8:16, lanes] = drag[0:8] + drag[8:16]

    def own_depth(k, carry):
        depth_block(k // cols + 2, k % cols + 2, k)
        return carry

    lax.fori_loop(0, rows * cols, own_depth, 0, unroll=32)

    if with_bound:
        pair_copy = pltpu.make_async_copy(pair_ref, pair_all, copies.at[2])
        pair_copy.start()

    def side_depth(c, carry):
        depth_block(1, 1 + c, None, (c, (6, 7, 8)))
        depth_block(rows + 2, 1 + c, None, (tile.ring_cols + c, (0, 1, 2)))
        return carry

    lax.fori_loop(0, tile.ring_cols, side_depth, 0, unroll=10)

    def end_depth(k, carry):
        depth_block(2 + k, 1, None, (2 * tile.ring_cols + k, (2, 5, 8)))
        depth_block(2 + k, cols + 2, None, (2 * tile.ring_cols + rows + k, (0, 3, 6)))
        return carry

    lax.fori_loop(0, rows, end_depth, 0, unroll=4)

    if with_bound:
        side_copy = pltpu.make_async_copy(side_ref, side_all, copies.at[3])
        side_copy.start()

    def column_row(r, carry):
        east, north, state = place_of(r)
        inner = slice(LANES, LANES + ring_lanes)
        east, north, state = east[:, inner], north[:, inner], state[:, inner]
        size = state[4:5]
        deep = size * depth_ref[r - 1, 0:1]
        blank = jnp.zeros((2, ring_lanes), F32)
        first = [size, deep, size * east, size * north, deep * east, deep * north, blank]
        first = jnp.concatenate(first, axis=0)
        if with_bound:
            exact_ref[r - 1] = first
        heavy = pieces(first * (size * size))
        heavy_ref[r - 1] = jnp.concatenate(heavy, axis=0).astype(BF16)
        return carry

    lax.fori_loop(1, tile.ring_rows + 1, column_row, 0, unroll=6)

    if with_bound:
        place_copy.wait()
        cell_copy.wait()
        groups = place_ref.shape[1] // GROUP
        cell = cell_ref[...]
        local = cell.astype(F32) - shift_ref[...]
        east = place_ref[0:1] + (local[0:1] + (2.0 - tile.east_centre))
        north = place_ref[1:2] + (local[1:2] + (2.0 - tile.north_centre))
        lanes = place_ref.shape[1]
        extra = tile.depth - 24
        which = row_iota(extra, lanes).astype(F32)
        apart_row = jnp.abs(which - (local[0:1] + 1.0))
        apart_col = jnp.abs(which - tile.ring_rows - (local[1:2] + 1.0))
        apart = jnp.where(which < tile.ring_rows - 0.5, apart_row, apart_col)
        apart = jnp.where(which < tile.mask_rows - 0.5, apart, 0.0)
        masks = jnp.where(apart > 1.5, -FAR, 0.0)
        bound = jnp.concatenate([own_features(east, north), masks], axis=0)
        for group in range(groups):
            back_ref[group] = bound[:, group * GROUP : (group + 1) * GROUP].T.astype(BF16)

        def bound_group(group, carry):
            own = back_ref[group]
            totals = [jnp.zeros((GROUP, LANES), F32) for _ in range(3)]
            for r in range(tile.ring_rows):
                near = near_ref[r + 1, :, LANES : LANES + ring_lanes]
                close = jnp.maximum(jnp.dot(own, near, preferred_element_type=F32), 0.0)
                for c in range(tile.ring_cols):
                    lanes = slice(c * LANES, (c + 1) * LANES)
                    second = close[:, lanes] * close[:, lanes]
                    for which, row in enumerate((1, 4, 5)):
                        weight = exact_ref[r, row : row + 1, lanes]
                        totals[which] = totals[which] + second * weight
            for which in range(3):
                total_ref[which, pl.ds(pl.multiple_of(group * GROUP, GROUP), GROUP)] = totals[which]
            return carry

        lax.fori_loop(0, groups, bound_group, 0)
        merged = []
        for which in range(3):
            parts = []
            for group in range(lanes // LANES):
                parts.append(lane_sums(total_ref[which, group * LANES : (group + 1) * LANES]))
            merged.append(jnp.concatenate(parts, axis=1))
        factor = 6.0 * gravity / LANES
        force_east = factor * (east * merged[0] - merged[1])
        force_north = factor * (north * merged[0] - merged[2])
        cell_place = cell.astype(F32)
        torque = (cell_place[0:1] + place_ref[0:1]) * force_north
        torque = torque - (cell_place[1:2] + place_ref[1:2]) * force_east
        chosen = row_iota(8, lanes) == slot_ref[...]
        columns = []
        for values in (force_east, force_north, torque):
            picked = jnp.where(chosen, jnp.broadcast_to(values, (8, lanes)), 0.0)
            columns.append(jnp.sum(picked, axis=1, keepdims=True))
        lane = lax.broadcasted_iota(jnp.int32, (8, LANES), 1)
        result = jnp.where(lane == 0, columns[0], jnp.where(lane == 1, columns[1], columns[2]))
        sums_out[...] = result
        pair_copy.wait()
        side_copy.wait()


def push_half(tile, wide_ref, kept, state_out, final_out=None, row_copy=None):
    depth_ref, pair_ref, side_ref, heavy_ref, sums_ref = kept
    rows, cols = tile.rows, tile.cols
    north_of = lane_block(tile.wide_cols * LANES).astype(F32) - tile.north_centre

    def place_of(r):
        state = wide_ref[r]
        east_shift = jnp.asarray(r, F32) - tile.east_centre
        return state[0:1] + east_shift, state[1:2] + north_of, state

    def weights_from(r, c, e, f):
        from_row, from_col = r + e, c + f
        if 1 <= from_row <= rows and 1 <= from_col <= cols:
            ref, index = pair_ref, (from_row - 1) * cols + from_col - 1
            place, places = (2 - e) * 3 + 2 - f, 9
        elif from_row in (0, rows + 1):
            ref, index = side_ref, from_col + (tile.ring_cols if from_row else 0)
            place, places = 2 - f, 3
        else:
            ref, index = side_ref, 2 * tile.ring_cols + from_row - 1 + (rows if from_col else 0)
            place, places = 2 - e, 3
        high = ref[index, :, place * LANES : (place + 1) * LANES]
        low = ref[index, :, (places + place) * LANES : (places + place + 1) * LANES]
        return high, low

    def push_block(r, c):
        lanes = slice(c * LANES, (c + 3) * LANES)
        near = [heavy_ref[r + e, :, lanes] for e in range(3)]
        highs, lows = zip(*[weights_from(r, c, e, f) for e in range(3) for f in range(3)])
        weights = jnp.concatenate(highs + lows, axis=0)
        total = jnp.dot(jnp.concatenate(near + near, axis=1), weights, preferred_element_type=F32)
        merged = total[0:8] + total[8:16] + total[16:24]
        sums_ref[r, 0:8, c * LANES : (c + 1) * LANES] = merged

    for r in range(rows):
        if final_out is not None:
            for step in {0: range(min(2, rows) + 1), rows - 1: ()}.get(r, (r + 2,)):
                row_copy(step).wait()
        for c in range(cols):
            push_block(r, c)

    def update_row(r, carry):
        east, north, state = place_of(r + 2)
        inner = slice(2 * LANES, (2 + cols) * LANES)
        east, north, state = east[:, inner], north[:, inner], state[:, inner]
        drag = sums_ref[r, 8:16]
        sums = sums_ref[r, 0:8] / (state[4:5] * state[4:5])
        depth = depth_ref[r + 1, 0:1, LANES : (1 + cols) * LANES]
        speed_east, speed_north = state[2:3], state[3:4]
        heavy = depth * sums[0:1] + sums[1:2]
        push_east = heavy * east - depth * sums[2:3] - sums[4:5]
        push_north = heavy * north - depth * sums[3:4] - sums[5:6]
        drag_east = drag[0:1] - speed_east * drag[2:3]
        drag_north = drag[1:2] - speed_north * drag[2:3]
        scale = 3.0 * gravity / LANES
        thin = viscosity / LANES
        speed_east = speed_east + step_time * (scale * push_east + thin * drag_east)
        speed_north = speed_north + step_time * (scale * push_north + thin * drag_north)
        east = state[0:1] + step_time * speed_east
        north = state[1:2] + step_time * speed_north
        if state_out is not None:
            blank = jnp.zeros((STATE_ROWS - 5, cols * LANES), F32)
            new = [east, north, speed_east, speed_north, state[4:5], blank]
            state_out[r] = jnp.concatenate(new, axis=0)
        else:
            position_out, velocity_out, depth_out = final_out
            for c in range(cols):
                lanes = slice(c * LANES, (c + 1) * LANES)
                position_out[r, 0, c : c + 1] = east[:, lanes]
                position_out[r, 1, c : c + 1] = north[:, lanes]
                velocity_out[r, 0, c : c + 1] = speed_east[:, lanes]
                velocity_out[r, 1, c : c + 1] = speed_north[:, lanes]
                depth_out[r, c : c + 1] = depth[:, lanes]
        return carry

    lax.fori_loop(0, rows, update_row, 0, unroll=4)


def kept_shapes(tile):
    rows, cols = tile.rows, tile.cols
    return [
        ((tile.ring_rows, 8, tile.ring_cols * LANES), F32),
        ((rows * cols, LANES, 18 * LANES), BF16),
        ((2 * (tile.ring_cols + rows), LANES, 6 * LANES), BF16),
        ((tile.ring_rows, 24, tile.ring_cols * LANES), BF16),
        ((rows, 16, cols * LANES), F32),
    ]


def scratch_shapes(tile):
    return [
        ((tile.wide_rows, tile.depth, tile.wide_cols * LANES), BF16),
        ((tile.ring_rows, tile.ring_cols, LANES, 32), BF16),
        ((tile.ring_rows, 16, tile.ring_cols * LANES), BF16),
    ]


def in_vmem(shapes):
    return [pltpu.VMEM(shape, dtype) for shape, dtype in shapes]


VMEM_SPEC = pl.BlockSpec(memory_space=pltpu.VMEM)
LIMIT = 52 << 20


def run_substep(tile, wide):
    def body(wide_ref, state_out, *refs):
        kept, scratch = refs[:5], refs[5:]
        depth_half(tile, wide_ref, None, kept, scratch)
        push_half(tile, wide_ref, kept, state_out)

    return pl.pallas_call(
        body,
        out_shape=jax.ShapeDtypeStruct((tile.rows, STATE_ROWS, tile.cols * LANES), F32),
        in_specs=[VMEM_SPEC],
        out_specs=VMEM_SPEC,
        scratch_shapes=in_vmem(kept_shapes(tile) + scratch_shapes(tile)),
        compiler_params=pltpu.CompilerParams(vmem_limit_bytes=LIMIT),
        name="substep",
    )(wide)


HBM_SPEC = pl.BlockSpec(memory_space=pltpu.HBM)


def in_hbm(array):
    return pltpu.with_memory_space_constraint(array, pltpu.HBM)


def run_bound(tile, wide, bound):
    place, cell, slot, shift = bound
    lanes = place.shape[1]
    back = [
        ((lanes // GROUP, GROUP, tile.depth), BF16),
        ((3, lanes, LANES), F32),
        ((tile.ring_rows, 8, tile.ring_cols * LANES), F32),
        (place.shape, F32),
        (cell.shape, jnp.int32),
    ]
    depth_shape, pair_shape, side_shape, heavy_shape, sums_shape = kept_shapes(tile)

    def body(wide_ref, place_all, cell_all, slot_ref, shift_ref, sums_out, *refs):
        depth_ref, pair_all, side_all, heavy_ref, sums_ref, pair_ref, side_ref = refs[:7]
        scratch, back_refs, copies = refs[7:10], refs[10:15], refs[15]
        bound_refs = back_refs[3:] + (slot_ref, shift_ref, sums_out) + back_refs[:3]
        bound_refs = bound_refs + (place_all, cell_all, pair_all, side_all, copies)
        kept_refs = (depth_ref, pair_ref, side_ref, heavy_ref, sums_ref)
        depth_half(tile, wide_ref, bound_refs, kept_refs, scratch)

    outs = [((8, LANES), F32), depth_shape, pair_shape, side_shape, heavy_shape, sums_shape]
    return pl.pallas_call(
        body,
        out_shape=[jax.ShapeDtypeStruct(shape, dtype) for shape, dtype in outs],
        in_specs=[VMEM_SPEC, HBM_SPEC, HBM_SPEC, VMEM_SPEC, VMEM_SPEC],
        out_specs=[VMEM_SPEC, VMEM_SPEC, HBM_SPEC, HBM_SPEC, VMEM_SPEC, VMEM_SPEC],
        scratch_shapes=in_vmem([pair_shape, side_shape] + scratch_shapes(tile) + back)
        + [pltpu.SemaphoreType.DMA((4,))],
        compiler_params=pltpu.CompilerParams(vmem_limit_bytes=LIMIT),
        name="depth_bound",
    )(wide, in_hbm(place), in_hbm(cell), slot, shift)


def run_push(tile, wide, kept):
    rows, cols = tile.rows, tile.cols
    pair = jax.ShapeDtypeStruct((rows, 2, cols, LANES), F32)
    kept_in = kept_shapes(tile)

    def body(wide_ref, depth_ref, pair_all, side_all, heavy_ref, drag_sums, *refs):
        position, velocity, depth, pair_ref, side_ref, sums_ref, copies = refs

        def row_copy(step):
            if step == 0:
                return pltpu.make_async_copy(side_all, side_ref, copies.at[0])
            part = pl.ds((step - 1) * cols, cols)
            return pltpu.make_async_copy(pair_all.at[part], pair_ref.at[part], copies.at[step])

        for step in range(rows + 1):
            row_copy(step).start()
        sums_ref[...] = drag_sums[...]
        kept_refs = (depth_ref, pair_ref, side_ref, heavy_ref, sums_ref)
        push_half(tile, wide_ref, kept_refs, None, (position, velocity, depth), row_copy)

    return pl.pallas_call(
        body,
        out_shape=[pair, pair, jax.ShapeDtypeStruct((rows, cols, LANES), F32)],
        in_specs=[VMEM_SPEC, VMEM_SPEC, HBM_SPEC, HBM_SPEC, VMEM_SPEC, VMEM_SPEC],
        out_specs=[VMEM_SPEC] * 3,
        scratch_shapes=in_vmem([kept_in[1], kept_in[2], kept_in[4]])
        + [pltpu.SemaphoreType.DMA((rows + 1,))],
        compiler_params=pltpu.CompilerParams(vmem_limit_bytes=40 << 20),
        cost_estimate=pl.CostEstimate(flops=8 * 10**9, bytes_accessed=2 * 10**7, transcendentals=0),
        name="push",
    )(wide, kept[0], in_hbm(kept[1]), in_hbm(kept[2]), *kept[3:])


def swapped_edges(low_edge, high_edge, axis):
    count = lax.axis_size(axis)
    odd = lax.axis_index(axis) % 2 == 1
    first = [(i, i ^ 1) for i in range(count)]
    second = [(i, ((i + 1) ^ 1) - 1) for i in range(1, count - 1)]
    to_first = jnp.where(odd, low_edge, high_edge)
    to_second = jnp.where(odd, high_edge, low_edge)
    from_first = lax.ppermute(to_first, axis, first)
    from_second = lax.ppermute(to_second, axis, second)
    low = jnp.where(odd, from_first, from_second)
    high = jnp.where(odd, from_second, from_first)
    return low, high


def with_halo(state):
    side = 2 * LANES
    low, high = swapped_edges(state[:, :, :side], state[:, :, -side:], ALONG_Y)
    state = jnp.concatenate([low, state, high], axis=2)
    low, high = swapped_edges(state[:2], state[-2:], "gx")
    return jnp.concatenate([low, state, high], axis=0)


def initial_state(position, velocity, volume):
    rows, _, cols, lanes = position.shape

    def body(position_ref, velocity_ref, volume_ref, state_out):
        blank = jnp.zeros((STATE_ROWS - 5, LANES), F32)
        for r in range(rows):
            volumes = volume_ref[r]
            size = jnp.exp(jnp.log(volumes) * (1.0 / 3.0))
            square = size * size
            size = size - (square * size - volumes) / (3.0 * square)
            for c in range(cols):
                row = slice(c, c + 1)
                new = [
                    position_ref[r, 0, row],
                    position_ref[r, 1, row],
                    velocity_ref[r, 0, row],
                    velocity_ref[r, 1, row],
                    size[row],
                    blank,
                ]
                state_out[r, :, c * LANES : (c + 1) * LANES] = jnp.concatenate(new, axis=0)

    return pl.pallas_call(
        body,
        out_shape=jax.ShapeDtypeStruct((rows, STATE_ROWS, cols * lanes), F32),
        in_specs=[VMEM_SPEC] * 3,
        out_specs=VMEM_SPEC,
        name="initial",
    )(position, velocity, volume)


def on_device(
    fluid_position,
    fluid_velocity,
    fluid_volume,
    bound_offset,
    bound_cell,
    bound_body,
    body_state,
    mass_inverse,
    inertia_inverse,
):
    rows, cols = fluid_position.shape[0], fluid_position.shape[2]
    tile = Tile(rows, cols)
    shard_bodies = body_state.shape[1]
    owners = lax.axis_size("body")
    devices = lax.axis_size(EVERY)
    tiles_north = lax.axis_size(ALONG_Y)
    body_total = shard_bodies * owners
    own_bodies = body_total // devices
    sharing = devices // owners
    me = lax.axis_index(EVERY)

    state = initial_state(fluid_position, fluid_velocity, fluid_volume)
    shift = jnp.stack([lax.axis_index("gx") * rows, lax.axis_index(ALONG_Y) * cols])
    shift = shift.astype(F32)[:, None]
    slot = bound_body - me * own_bodies
    slot = jnp.where(slot < 0, slot + 2 * own_bodies, slot)

    bodies = jnp.concatenate([body_state, mass_inverse[None], inertia_inverse[None]], axis=0)
    by_home = bodies.reshape(7, sharing, own_bodies)
    place = lax.broadcasted_iota(jnp.int32, (1, sharing, 1), 1) % tiles_north
    after = jnp.concatenate([by_home[:, 1:], by_home[:, -1:]], axis=1)
    before = jnp.concatenate([by_home[:, :1], by_home[:, :-1]], axis=1)
    beside = jnp.where(place == tiles_north - 1, before, after)
    params = jnp.concatenate([by_home, beside], axis=2)
    params = jnp.transpose(params, (1, 0, 2)).reshape(sharing, 7 * 2 * own_bodies)
    params = jnp.concatenate([params] * owners, axis=0)

    def whole_substep(_, state):
        return run_substep(tile, with_halo(state))

    state = lax.fori_loop(0, SUBSTEPS - 1, whole_substep, state)
    bound = (bound_offset, bound_cell, slot[None], shift)
    wide = with_halo(state)
    sums, *kept = run_bound(tile, wide, bound)

    partial = sums[:, :3].T.reshape(1, 6 * own_bodies)
    message = jnp.concatenate([jnp.broadcast_to(partial, (devices, 6 * own_bodies)), params], axis=1)
    received = lax.all_to_all(message, EVERY, 0, 0, tiled=True)
    position, velocity, depth = run_push(tile, wide, kept)
    partials = received[:, : 6 * own_bodies].reshape(devices, 3, 2 * own_bodies)
    partials = jnp.transpose(partials, (1, 0, 2))
    own_part, beside_part = partials[:, :, :own_bodies], partials[:, :, own_bodies:]
    place = lax.broadcasted_iota(jnp.int32, (1, devices, 1), 1) % tiles_north
    from_before = jnp.concatenate([beside_part[:, :1], beside_part[:, :-1]], axis=1)
    from_after = jnp.concatenate([beside_part[:, 1:], beside_part[:, -1:]], axis=1)
    totals = own_part + jnp.where(place > 0, from_before, 0.0)
    totals = totals + jnp.where(place == tiles_north - 2, from_after, 0.0)

    def integrate(state_of, mass_of, inertia_of, sums_of):
        span = step_time * SUBSTEPS
        east = state_of[2] + span * mass_of * sums_of[0]
        north = state_of[3] + span * mass_of * sums_of[1]
        torque = sums_of[2] - (state_of[0] * sums_of[1] - state_of[1] * sums_of[0])
        return jnp.stack([east, north, state_of[4] + span * inertia_of * torque])

    shard = lax.axis_index("body")
    shard_sums = lax.dynamic_slice_in_dim(totals, shard * sharing, sharing, axis=1)
    shard_sums = shard_sums.reshape(3, shard_bodies)
    motion = integrate(body_state, mass_inverse, inertia_inverse, shard_sums)

    tile_place = lax.axis_index(ALONG_Y)
    other = jnp.where(tile_place == tiles_north - 1, me - 1, me + 1)
    mine = lax.dynamic_slice_in_dim(totals, me, 1, axis=1)[:, 0]
    theirs = lax.dynamic_slice_in_dim(totals, other, 1, axis=1)[:, 0]
    local_sums = jnp.concatenate([mine, theirs], axis=1)
    local = lax.dynamic_slice_in_dim(received, me // sharing, 1, axis=0)[0, 6 * own_bodies :]
    local = local.reshape(7, 2 * own_bodies)
    local_motion = integrate(local[:5], local[5], local[6], local_sums)
    table = jnp.concatenate([local_motion, local[:2]], axis=0)
    chosen = slot[None, :, None] == jnp.arange(2 * own_bodies, dtype=jnp.int32)
    picked = jnp.sum(jnp.where(chosen, table[:, None, :], 0.0), axis=-1)
    place_east = bound_cell[0].astype(F32) + bound_offset[0]
    place_north = bound_cell[1].astype(F32) + bound_offset[1]
    bound_velocity = jnp.stack(
        [
            picked[0] - picked[2] * (place_north - picked[4]),
            picked[1] + picked[2] * (place_east - picked[3]),
        ]
    )
    return position, velocity, depth, motion, bound_velocity


def solution(mesh):
    return jax.shard_map(
        on_device,
        mesh=mesh,
        in_specs=(
            P("gx", None, ("gy", "body"), None),
            P("gx", None, ("gy", "body"), None),
            P("gx", ("gy", "body"), None),
            P(None, ("gx", "gy", "body")),
            P(None, ("gx", "gy", "body")),
            P(("gx", "gy", "body")),
            P(None, "body"),
            P("body"),
            P("body"),
        ),
        out_specs=(
            P("gx", None, ("gy", "body"), None),
            P("gx", None, ("gy", "body"), None),
            P("gx", ("gy", "body"), None),
            P(None, "body"),
            P(None, ("gx", "gy", "body")),
        ),
        check_vma=False,
    )
```
